512 devices in a mesh: subj: 128 (over z, x_hi, y), feat: 4 (over x_lo, core).
Axes of the slice: x: 4 (x_hi: 2, x_lo: 2; x = x_hi * 2 + x_lo), y: 8, z: 8, core: 2. Of those that a mesh axis runs over, the one named last changes fastest.
Arguments:
- visits: bfloat16 [1024, 56, 10240], P('subj', None, 'feat'), may hold values from -6 to 6
- tile_pattern: int32 [1024, 80], P('subj', 'feat'), may hold values 0 or 1
- counts: int32 [1024], P('subj'), may hold values from 1 to 56, 28672 in all
- codes_t: bfloat16 [256, 10240], P('subj', 'feat'), may hold values from -0.0625 to 0.0625
- core: bfloat16 [256, 256], replicated, may hold values from -0.375 to 0.375
- patient_weights: float32 [1024, 256], P('subj'), may hold values from 0.3 to 3
Outputs:
- code_mttkrp: float32 [256, 10240], P('subj', 'feat')
- patient_mttkrp: float32 [1024, 256], P('subj')
The draws below stay inside these ranges and needn't reach their ends.
Inputs may be any that keep to these rules, and one draw needn't show every extreme that they name: `counts`: every patient has at least one visit; some patient has exactly 56.
All inputs are finite; a program needn't handle non-finite values. No bound on the sum of `tile_pattern` or of `counts` on one device may be relied on, other than what follows from the above.
Results may differ from the reference program's by a relative error of at most 0.0019.
Values may be sent and summed in bfloat16 or wider, within the bound.
A program may use at most 64 MiB of HBM per device.

```python
import math
import jax
import jax.numpy as jnp
import numpy as np
from jax import lax

R = 256
J = 10240
TILE = 128
MAXV = 56
PAT_DEV = 8
NS_STEPS = 8
PATIENTS = 1024
CODE_TILES = 80


def place_ends(entries, stream_key, least, high):
    longest = entries.shape.index(max(entries.shape))
    spots = []
    for shift in (0, 1):
        where = [jax.random.randint(jax.random.fold_in(stream_key, axis), (), 0, length) for axis, length in enumerate(entries.shape)]
        where[longest] = (where[longest] + shift) % entries.shape[longest]
        spots.append(tuple(where))
    return entries.at[spots[0]].set(least).at[spots[1]].set(high)


def block_scale(rng, extent, pieces, smallest, high):
    def one(axis_at, parts):
        steps = jax.random.uniform(jax.random.fold_in(jax.random.fold_in(rng, 6), axis_at), (parts,), jnp.float32, smallest / len(pieces), high / len(pieces))
        return jnp.repeat(jnp.exp(steps), extent[axis_at] // parts).reshape((-1,) + (1,) * (len(extent) - axis_at - 1))

    level = one(*pieces[0])
    for cut in pieces[1:]:
        level = level * one(*cut)
    return level


def split_up(number_of, total, most, skew):
    loads = [(1 << 20) // math.isqrt(standing ** skew) + 1 for standing in range(2, number_of + 1)]
    spare, given = total - most - (number_of - 1), [1] * (number_of - 1)
    while spare > 0:
        movable = [i for i in range(number_of - 1) if given[i] < most]
        mass, remaining = sum([loads[i] for i in movable]), spare
        for i in movable:
            more = min(most - given[i], max(1, remaining * loads[i] // mass), spare)
            given[i] = given[i] + more
            spare = spare - more
    return np.array([most] + given)


def uneven(key, number_of, total, reach, slope):
    if number_of == 2:
        one = jax.random.randint(key, (), max(1, total - reach), min(reach, total - 1) + 1)
        return jnp.stack([one, total - one])
    sizes = jnp.asarray(split_up(number_of, total, reach, slope), jnp.int32)
    pairs = (number_of - 1) // 2
    giver, sink = sizes[1:1 + 2 * pairs:2], sizes[2:2 + 2 * pairs:2]
    slack = jnp.minimum(giver - 1, reach - sink)
    moved = jax.random.randint(jax.random.fold_in(key, 1), (pairs,), 0, 1 << 20) % (slack + 1)
    sizes = sizes.at[1:1 + 2 * pairs:2].set(giver - moved).at[2:2 + 2 * pairs:2].set(sink + moved)
    return sizes[jax.random.permutation(jax.random.fold_in(key, 2), number_of)]


def bell_draw(stream_key, dims, spread, most, shards=(), kind=jnp.bfloat16):
    array = jax.random.normal(stream_key, dims, jnp.float32) * spread
    if len(shards) > 0:
        array = block_scale(stream_key, dims, shards, -0.22, 0.18) * array
    return jnp.clip(array, min=-most, max=most).astype(kind)


def setup_inputs(seed: int = 0) -> dict:
    arg_keys = jax.random.split(jax.random.key(seed), 7)
    visits = bell_draw(arg_keys[0], (PATIENTS, MAXV, J), 1.0, 6.0, ((0, 128), (2, 4)))
    tile_pattern = place_ends((jax.random.randint(arg_keys[1], (PATIENTS, CODE_TILES), 0, 2) < 1).astype(jnp.int32), jax.random.fold_in(arg_keys[1], 1), 0, 1)
    counts = uneven(arg_keys[2], PATIENTS, PATIENTS * MAXV // 2, MAXV, 1).astype(jnp.int32)
    codes_t = bell_draw(arg_keys[3], (R, J), J ** -0.5, 0.0625, ((0, 128), (1, 4)))
    core = bell_draw(arg_keys[4], (R, R), R ** -0.5, 0.375)
    patient_weights = jnp.clip(jnp.exp(math.log(3.0) - 2.3025851 * jax.random.uniform(arg_keys[5], (PATIENTS, R), jnp.float32) ** block_scale(arg_keys[5], (PATIENTS, R), ((0, 128),), -0.2, 0.2)), 0.3, 3.0)
    return dict(visits=visits, tile_pattern=tile_pattern, counts=counts, codes_t=codes_t, core=core, patient_weights=patient_weights)


def procrustes(projected, weights, core_f):
    scaled = projected * weights[:, None, :]
    target = jnp.einsum('pir,sr->pis', scaled, core_f, precision=lax.Precision.HIGHEST)
    total = lax.optimization_barrier(jnp.sum(target * target, axis=(1, 2)))
    rotation = target * lax.rsqrt(total + 1e-06)[:, None, None]
    for step in range(NS_STEPS):
        gram = jnp.einsum('pis,pks->pik', rotation, rotation, precision=lax.Precision.HIGHEST)
        rotation = 1.5 * rotation - 0.5 * jnp.einsum('pik,pks->pis', gram, rotation, precision=lax.Precision.HIGHEST)
    rotated = jnp.einsum('pis,sr->pir', rotation, core_f, precision=lax.Precision.HIGHEST)
    patient_rows = lax.optimization_barrier(jnp.sum(rotated * projected, axis=1))
    weighted = (rotated * weights[:, None, :]).astype(jnp.bfloat16)
    return (weighted, patient_rows)

def reference(visits, tile_pattern, counts, codes_t, core, patient_weights):
    core_f = core.astype(jnp.float32)
    blocks = PATIENTS // PAT_DEV
    visit_blocks = visits.reshape(blocks, PAT_DEV, MAXV, J)
    pattern_blocks = tile_pattern.reshape(blocks, PAT_DEV, CODE_TILES)
    count_blocks = counts.reshape(blocks, PAT_DEV)
    weight_blocks = patient_weights.reshape(blocks, PAT_DEV, R)

    def advance(total, block):
        values, pattern, lengths, weights = block
        live = (lax.broadcasted_iota(jnp.int32, (PAT_DEV, MAXV), 1) < lengths[:, None]).astype(jnp.int32)
        gate = (pattern[:, None, :, None] * live[:, :, None, None]).astype(jnp.bfloat16)
        masked = (values.reshape(PAT_DEV, MAXV, CODE_TILES, TILE) * gate).reshape(PAT_DEV * MAXV, J)
        projected = lax.dot_general(masked, codes_t, (((1,), (1,)), ((), ())), preferred_element_type=jnp.float32)
        weighted, patient_rows = procrustes(projected.reshape(PAT_DEV, MAXV, R), weights, core_f)
        term = lax.dot_general(weighted.reshape(PAT_DEV * MAXV, R), masked, (((0,), (0,)), ((), ())), preferred_element_type=jnp.float32)
        return (total + term, patient_rows)
    total, rows = lax.scan(advance, jnp.zeros((R, J), jnp.float32), (visit_blocks, pattern_blocks, count_blocks, weight_blocks))
    return (total, rows.reshape(PATIENTS, R))
```

```python
import functools

import jax
import jax.numpy as jnp
from jax import lax
from jax.experimental import pallas as pl
from jax.experimental.pallas import tpu as pltpu
from jax.sharding import PartitionSpec as P

NS_STEPS = 8
NZ, NX, NY = 8, 2, 8
VP = 64
QMAX = 32000.0
F32 = jnp.float32
BF16 = jnp.bfloat16
I16 = jnp.int16
NT = (((1,), (1,)), ((), ()))


def split2(x):
    hi = x.astype(BF16)
    lo = (x - hi.astype(F32)).astype(BF16)
    return hi, lo


def left3(x):
    hi, lo = split2(x)
    return jnp.concatenate([hi, lo, hi], axis=1)


def right3(x):
    hi, lo = split2(x)
    return jnp.concatenate([hi, hi, lo], axis=0)


def mm(a, b):
    return jnp.dot(a, b, preferred_element_type=F32)


def quant(v):
    top = jnp.max(jnp.max(jnp.abs(v), axis=0, keepdims=True), axis=1, keepdims=True)
    top = jnp.maximum(top, 1e-30)
    q = jnp.round(v * (QMAX / top)).astype(jnp.int32).astype(I16)
    return q, top * (1.0 / QMAX)


def dequant(q, scale):
    return q.astype(jnp.int32).astype(F32) * scale


def kernel(
    dims,
    visits_ref, pat_ref, cnt_ref, codes_ref, core_ref, pw_ref,
    out_codes, out_pat,
    vis, mk, xbuf, ga, gb, rel, ca, cb, projf, ra, rb, sb, wbuf, prow, wt, ta, tb,
    qs_a, qr_a, qs_b, qr_b, fs_a, fr_a, fs_b, fr_b, s2a, r2a, s2b, r2b, xs, xr,
    lsem, xsem, g1sem, ringsem, featsem, wsem, psem, rsem, rssem, g2sem, xfsem,
):
    nz, nx, ny = dims
    npat, nvis, ncode = visits_ref.shape
    rank = core_ref.shape[0]
    half = ncode // 2
    ntile = pat_ref.shape[1]
    tile = ncode // ntile
    subj = lax.axis_index("subj")
    feat = lax.axis_index("feat")
    z = subj // (nx * ny)
    xh = (subj // ny) % nx
    y = subj % ny
    xlo, core = feat // 2, feat % 2

    def at(zz, xx, yy, ff):
        return {"subj": (zz * nx + xx) * ny + yy, "feat": ff}

    def zdev(d):
        return at((z + d + nz) % nz, xh, y, feat)

    def ydev(d):
        return at(z, xh, (y + d + ny) % ny, feat)

    xdev = at(z, 1 - xh, y, feat)

    def fdev(d):
        return at(z, xh, y, (feat + d) % 4)

    def remote(src, dst, sems, i, dev):
        return pltpu.make_async_remote_copy(
            src_ref=src, dst_ref=dst, send_sem=sems.at[0, i], recv_sem=sems.at[1, i],
            device_id=dev, device_id_type=pl.DeviceIdType.MESH,
        )

    load = pltpu.make_async_copy(visits_ref, vis, lsem)
    load.start()
    barrier = pltpu.get_barrier_semaphore()
    partners = (
        [xdev] + [fdev(d) for d in range(1, 4)]
        + [ydev(d) for d in range(1, ny)] + [zdev(d) for d in range(1, nz)]
    )
    for dev in partners:
        pl.semaphore_signal(barrier, inc=1, device_id=dev, device_id_type=pl.DeviceIdType.MESH)
    pl.semaphore_wait(barrier, len(partners))

    xcopy = remote(codes_ref, xbuf.at[xh], xsem, 0, xdev)
    xcopy.start()
    xbuf[xh] = codes_ref[...]
    xcopy.wait()
    g1 = []
    for d in range(1, ny):
        g1.append(remote(xbuf.at[:, :, pl.ds(0, half)], ga.at[:, y], g1sem, d, ydev(d)))
    for d in range(1, nz):
        g1.append(remote(xbuf.at[:, :, pl.ds(half, half)], gb.at[z], g1sem, ny + d, zdev(d)))
    for c in g1:
        c.start()
    for j in range(nx):
        ga[j, y] = xbuf[j, :, 0:half]
        gb[z, j] = xbuf[j, :, half:ncode]

    load.wait()
    mk[:, nvis:, :] = jnp.zeros((npat, VP - nvis, ncode), BF16)

    def mask_patient(k, carry):
        for t in range(ntile):
            cols = slice(t * tile, (t + 1) * tile)
            v = vis[k, :, cols]
            mk[k, 0:nvis, cols] = jnp.where(pat_ref[k, t] > 0, v, jnp.zeros_like(v))
        return carry

    lax.fori_loop(0, npat, mask_patient, 0)

    for c in g1:
        c.wait_recv()
    for s in range(nx * ny):
        rel[2 * s : 2 * s + 2, :] = ga[s // ny, s % ny].astype(F32)
    ca[z] = rel[0 : 2 * nx * ny, :].astype(BF16)
    for s in range(nz * nx):
        rel[2 * s : 2 * s + 2, :] = gb[s // nx, s % nx].astype(F32)
    cb[y] = rel[0 : 2 * nz * nx, :].astype(BF16)

    rings = ((ca, z, nz, zdev, 0), (cb, y, ny, ydev, 16))
    pending = list(g1)

    def ring_copy(buf, me, n, dev, base, way, t):
        slot = (me - way * t + n) % n
        off = base + (t if way > 0 else 8 + t)
        return remote(buf.at[slot], buf.at[slot], ringsem, off, dev(way))

    live = {}
    for buf, me, n, dev, base in rings:
        for way in (1, -1):
            steps = n // 2 if way > 0 else n - 1 - n // 2
            if steps:
                live[base, way] = ring_copy(buf, me, n, dev, base, way, 0)
                live[base, way].start()
    for t in range(1, max(nz, ny) // 2 + 1):
        for buf, me, n, dev, base in rings:
            for way in (1, -1):
                steps = n // 2 if way > 0 else n - 1 - n // 2
                if t > steps:
                    continue
                live[base, way].wait_recv()
                pending.append(live[base, way])
                if t < steps:
                    live[base, way] = ring_copy(buf, me, n, dev, base, way, t)
                    live[base, way].start()

    blk = 2 * nz * nx

    def natural(rp):
        yy, rest = rp // blk, rp % blk
        zx, i = rest // 2, rest % 2
        return (zx // nx) * (2 * nx * ny) + (zx % nx) * (2 * ny) + yy * 2 + i

    rows = lax.broadcasted_iota(jnp.int32, (rank, rank), 0)
    cols = lax.broadcasted_iota(jnp.int32, (rank, rank), 1)
    to_nat = jnp.where(rows == natural(cols), 1.0, 0.0).astype(BF16)
    to_b = jnp.where(natural(rows) == cols, 1.0, 0.0).astype(BF16)

    cbn = mm(to_nat, cb[...].reshape(rank, half)).astype(BF16)
    flat = npat * VP
    proj = lax.dot_general(
        mk[:, :, 0:half].reshape(flat, half), ca[...].reshape(rank, half), NT,
        preferred_element_type=F32,
    ) + lax.dot_general(
        mk[:, :, half:ncode].reshape(flat, half), cbn, NT, preferred_element_type=F32
    )
    own = flat // 4
    projf[...] = proj.reshape(2, 2, own, rank)

    fa = remote(projf.at[:, 1 - core], ra, featsem, 0, at(z, xh, y, xlo * 2 + 1 - core))
    fa.start()
    fa.wait()
    sb[...] = projf[1 - xlo, core] + ra[1 - xlo]
    fb = remote(sb, rb, featsem, 1, at(z, xh, y, (1 - xlo) * 2 + core))
    fb.start()
    mine = projf[xlo, core] + ra[xlo]
    fb.wait()
    projected = mine + rb[...]

    np_own = npat // 4
    rowi = lax.broadcasted_iota(jnp.int32, (own, rank), 0)
    limit = jnp.full((own, rank), cnt_ref[feat * np_own], jnp.int32)
    weights = jnp.broadcast_to(pw_ref[pl.ds(feat * np_own, 1), :], (own, rank))
    for p in range(1, np_own):
        here = rowi >= p * VP
        limit = jnp.where(here, cnt_ref[feat * np_own + p] + p * VP, limit)
        weights = jnp.where(here, pw_ref[pl.ds(feat * np_own + p, 1), :], weights)
    projected = jnp.where(rowi < limit, projected, 0.0)
    hi, lo = split2(projected * weights)
    core_w = core_ref[...]
    both = lax.dot_general(
        jnp.concatenate([hi, lo], axis=0), core_w, NT, preferred_element_type=F32
    )
    target = both[0:own] + both[own:]
    hi, lo = split2(target)
    gram = lax.dot_general(
        jnp.concatenate([hi, lo, hi], axis=1), jnp.concatenate([hi, hi, lo], axis=1), NT,
        preferred_element_type=F32,
    )
    both = mm(jnp.concatenate([hi, lo], axis=0), core_w)
    base = both[0:own] + both[own:]
    gi = lax.broadcasted_iota(jnp.int32, (own, own), 0)
    gj = lax.broadcasted_iota(jnp.int32, (own, own), 1)
    square = jnp.sum(target * target, axis=1, keepdims=True)
    scale = jnp.zeros((own, 1), F32)
    pi = lax.broadcasted_iota(jnp.int32, (own, 1), 0) // VP
    for p in range(np_own):
        total = jnp.sum(square[p * VP : (p + 1) * VP], axis=0, keepdims=True)
        scale = jnp.where(pi == p, lax.rsqrt(total + 1e-06), scale)
    gram = jnp.where(gi // VP == gj // VP, gram * (scale * scale), 0.0)
    eye = jnp.where(gi == gj, 1.0, 0.0)
    base = base * scale

    def grow(g, right):
        half_step = 1.5 * g - 0.5 * mm(left3(g), right)
        return 1.5 * half_step - 0.5 * mm(left3(half_step), right)

    poly = 1.5 * eye - 0.5 * gram
    gram = grow(gram, right3(gram))

    def ns_step(i, carry):
        poly, gram = carry
        right = right3(gram)
        return (1.5 * poly - 0.5 * mm(left3(poly), right), grow(gram, right))

    poly, gram = lax.fori_loop(0, NS_STEPS - 2, ns_step, (poly, gram))
    poly = 1.5 * poly - 0.5 * mm(left3(poly), right3(gram))
    rotated = mm(left3(poly), right3(base))
    prod = rotated * projected
    for p in range(np_own):
        prow[feat, p : p + 1, :] = jnp.sum(prod[p * VP : (p + 1) * VP], axis=0, keepdims=True)
    wbuf[feat] = (rotated * weights).T.astype(BF16)
    wcopies = []
    for d in range(1, 4):
        wcopies.append(remote(wbuf.at[feat], wbuf.at[feat], wsem, d, fdev(d)))
        wcopies.append(remote(prow.at[feat], prow.at[feat], psem, d, fdev(d)))
    for c in wcopies:
        c.start()
    for c in wcopies:
        c.wait_recv()
    pending += wcopies

    for f in range(4):
        wt[:, f * own : (f + 1) * own] = wbuf[f]
        out_pat[f * np_own : (f + 1) * np_own, :] = prow[f]
    ta[...] = mm(wt[...], mk[:, :, 0:half].reshape(flat, half)).reshape(ta.shape)
    wt_b = mm(to_b, wt[...]).astype(BF16)
    tb[...] = mm(wt_b, mk[:, :, half:ncode].reshape(flat, half)).reshape(tb.shape)

    sums = (
        (ta, z, nz, zdev, qs_a, qr_a, fs_a, fr_a, 0),
        (tb, y, ny, ydev, qs_b, qr_b, fs_b, fr_b, 16),
    )
    live = {}

    def arrived(key, qr, fr, slot):
        for c in live[key]:
            c.wait_recv()
        return dequant(qr[slot], fr[slot, :, 0:1])

    for t in range(max(nz, ny) // 2):
        for term, me, n, dev, qs, qr, fs, fr, off in sums:
            right = n // 2
            for way in (1, -1):
                steps = right if way > 0 else n - 1 - right
                if t >= steps:
                    continue
                slot = t if way > 0 else right + t
                v = term[(me + way * (steps - t) + n) % n]
                if t:
                    v = v + arrived((off, way), qr, fr, slot - 1)
                q, inv = quant(v)
                qs[slot] = q
                fs[slot] = jnp.broadcast_to(inv, fs.shape[1:])
                live[off, way] = (
                    remote(qs.at[slot], qr.at[slot], rsem, off + slot, dev(way)),
                    remote(fs.at[slot], fr.at[slot], rssem, off + slot, dev(way)),
                )
                for c in live[off, way]:
                    c.start()
                    pending.append(c)

    def ring_total(term, me, n, qr, fr, off):
        right = n // 2
        v = term[me] + arrived((off, 1), qr, fr, right - 1)
        if n - 1 - right:
            v = v + arrived((off, -1), qr, fr, n - 2)
        return v

    rel[0 : 2 * nx * ny, :] = ring_total(ta, z, nz, qr_a, fr_a, 0)
    for s in range(nx * ny):
        s2a[s % ny, s // ny] = rel[2 * s : 2 * s + 2, :]
    g2 = []
    for d in range(1, ny):
        to = (y + d) % ny
        g2.append(remote(s2a.at[to], r2a.at[y], g2sem, d, ydev(d)))
    for c in g2:
        c.start()
    rel[0 : 2 * nz * nx, :] = ring_total(tb, y, ny, qr_b, fr_b, 16)
    for s in range(nz * nx):
        s2b[s // nx, s % nx] = rel[2 * s : 2 * s + 2, :]
    g3 = []
    for d in range(1, nz):
        to = (z + d) % nz
        g3.append(remote(s2b.at[to], r2b.at[z], g2sem, ny + d, zdev(d)))
    for c in g3:
        c.start()
    pending += g2 + g3
    for c in g2:
        c.wait_recv()
    suma = s2a[y]
    for d in range(1, ny):
        suma = suma + r2a[(y + d) % ny]
    for c in g3:
        c.wait_recv()
    sumb = s2b[z]
    for d in range(1, nz):
        sumb = sumb + r2b[(z + d) % nz]
    xs[:, :, 0:half] = suma
    xs[:, :, half:ncode] = sumb
    xf = remote(xs.at[1 - xh], xr, xfsem, 0, xdev)
    xf.start()
    xf.wait()
    out_codes[...] = xs[xh] + xr[...]
    for c in pending:
        c.wait_send()


def per_device(visits, tile_pattern, counts, codes_t, core, patient_weights, dims):
    nz, nx, ny = dims
    npat, nvis, ncode = visits.shape
    rank = core.shape[0]
    half = ncode // 2
    rows_a, rows_b = 2 * nx * ny, 2 * nz * nx
    flat = npat * VP
    own = flat // 4
    dma = pltpu.SemaphoreType.DMA
    vmem = pl.BlockSpec(memory_space=pltpu.VMEM)
    smem = pl.BlockSpec(memory_space=pltpu.SMEM)
    scratch = [
        pltpu.VMEM((npat, nvis, ncode), BF16),
        pltpu.VMEM((npat, VP, ncode), BF16),
        pltpu.VMEM((nx, 2, ncode), BF16),
        pltpu.VMEM((nx, ny, 2, half), BF16),
        pltpu.VMEM((nz, nx, 2, half), BF16),
        pltpu.VMEM((max(rows_a, rows_b), half), F32),
        pltpu.VMEM((nz, rows_a, half), BF16),
        pltpu.VMEM((ny, rows_b, half), BF16),
        pltpu.VMEM((2, 2, own, rank), F32),
        pltpu.VMEM((2, own, rank), F32),
        pltpu.VMEM((own, rank), F32),
        pltpu.VMEM((own, rank), F32),
        pltpu.VMEM((4, rank, own), BF16),
        pltpu.VMEM((4, npat // 4, rank), F32),
        pltpu.VMEM((rank, flat), BF16),
        pltpu.VMEM((nz, rows_a, half), F32),
        pltpu.VMEM((ny, rows_b, half), F32),
        pltpu.VMEM((nz - 1, rows_a, half), I16),
        pltpu.VMEM((nz - 1, rows_a, half), I16),
        pltpu.VMEM((ny - 1, rows_b, half), I16),
        pltpu.VMEM((ny - 1, rows_b, half), I16),
        pltpu.VMEM((nz - 1, 1, 128), F32),
        pltpu.VMEM((nz - 1, 1, 128), F32),
        pltpu.VMEM((ny - 1, 1, 128), F32),
        pltpu.VMEM((ny - 1, 1, 128), F32),
        pltpu.VMEM((ny, nx, 2, half), F32),
        pltpu.VMEM((ny, nx, 2, half), F32),
        pltpu.VMEM((nz, nx, 2, half), F32),
        pltpu.VMEM((nz, nx, 2, half), F32),
        pltpu.VMEM((nx, 2, ncode), F32),
        pltpu.VMEM((2, ncode), F32),
        dma,
        dma((2, 1)),
        dma((2, ny + nz)),
        dma((2, 32)),
        dma((2, 2)),
        dma((2, 4)),
        dma((2, 4)),
        dma((2, 32)),
        dma((2, 32)),
        dma((2, ny + nz)),
        dma((2, 1)),
    ]
    return pl.pallas_call(
        functools.partial(kernel, dims),
        out_shape=(
            jax.ShapeDtypeStruct(codes_t.shape, F32),
            jax.ShapeDtypeStruct(patient_weights.shape, F32),
        ),
        in_specs=[pl.BlockSpec(memory_space=pl.ANY), smem, smem, vmem, vmem, vmem],
        out_specs=(vmem, vmem),
        scratch_shapes=scratch,
        compiler_params=pltpu.CompilerParams(
            collective_id=0, has_side_effects=True, vmem_limit_bytes=48 * 1024 * 1024
        ),
        name="sweep",
    )(visits, tile_pattern, counts, codes_t, core, patient_weights)


def build(mesh, dims):
    return jax.shard_map(
        functools.partial(per_device, dims=dims),
        mesh=mesh,
        in_specs=(
            P("subj", None, "feat"),
            P("subj", "feat"),
            P("subj"),
            P("subj", "feat"),
            P(),
            P("subj", None),
        ),
        out_specs=(P("subj", "feat"), P("subj", None)),
        check_vma=False,
    )


def solution(mesh):
    return build(mesh, (NZ, NX, NY))
```

```python
import functools

import jax
import jax.numpy as jnp
from jax import lax
from jax.experimental import pallas as pl
from jax.experimental.pallas import tpu as pltpu
from jax.sharding import PartitionSpec as P

NS_STEPS = 8
NZ, NX, NY = 8, 2, 8
VP = 64
QMAX = 32000.0
F32 = jnp.float32
BF16 = jnp.bfloat16
I16 = jnp.int16
NT = (((1,), (1,)), ((), ()))


def split2(x):
    hi = x.astype(BF16)
    lo = (x - hi.astype(F32)).astype(BF16)
    return hi, lo


def left3(x):
    hi, lo = split2(x)
    return jnp.concatenate([hi, lo, hi], axis=1)


def right3(x):
    hi, lo = split2(x)
    return jnp.concatenate([hi, hi, lo], axis=0)


def mm(a, b):
    return jnp.dot(a, b, preferred_element_type=F32)


def tiles(v):
    return [v[:, c : c + 128] for c in range(0, v.shape[1], 128)]


def quant(v):
    parts = tiles(v)
    top = jnp.abs(parts[0])
    for part in parts[1:]:
        top = jnp.maximum(top, jnp.abs(part))
    exponent = jnp.floor(jnp.log2(jnp.maximum(top, 1e-30))) + 1.0
    scale = jnp.exp2(-exponent) * QMAX
    codes = [jnp.round(part * scale) for part in parts] + [exponent]
    return jnp.concatenate(codes, axis=1).astype(jnp.int32).astype(I16)


def dequant(q):
    parts = tiles(q.astype(jnp.int32).astype(F32))
    scale = jnp.exp2(parts[-1]) * (1.0 / QMAX)
    return jnp.concatenate([part * scale for part in parts[:-1]], axis=1)


def kernel(
    dims,
    visits_in, pat_in, cnt_in, codes_in, core_in, pw_in,
    out_codes, out_pat,
    vis, pat_ref, cnt_ref, core_ref, pw_ref, mk, xbuf, ga, gb, rel, ca, cb, projf, ra, rb, sb, wbuf, prow, wt, ta, tb,
    qs, qr, s2a, r2a, s2b, r2b, xs, xr,
    lsem, xsem, g1sem, ringsem, featsem, wsem, psem, rsem, g2sem, xfsem,
):
    nz, nx, ny = dims
    npat, nvis, ncode = visits_in.shape
    rank = core_ref.shape[0]
    half = ncode // 2
    ntile = pat_ref.shape[1]
    tile = ncode // ntile
    subj = lax.axis_index("subj")
    feat = lax.axis_index("feat")
    z = subj // (nx * ny)
    xh = (subj // ny) % nx
    y = subj % ny
    xlo, core = feat // 2, feat % 2

    def at(zz, xx, yy, ff):
        return {"subj": (zz * nx + xx) * ny + yy, "feat": ff}

    def zdev(d):
        return at((z + d + nz) % nz, xh, y, feat)

    def ydev(d):
        return at(z, xh, (y + d + ny) % ny, feat)

    xdev = at(z, 1 - xh, y, feat)

    def fdev(d):
        return at(z, xh, y, (feat + d) % 4)

    def remote(src, dst, sems, i, dev):
        return pltpu.make_async_remote_copy(
            src_ref=src, dst_ref=dst, send_sem=sems.at[0, i], recv_sem=sems.at[1, i],
            device_id=dev, device_id_type=pl.DeviceIdType.MESH,
        )

    loads = [
        pltpu.make_async_copy(src, dst, lsem.at[i])
        for i, (src, dst) in enumerate((
            (codes_in, xbuf.at[xh]), (pat_in, pat_ref), (visits_in, vis),
            (cnt_in, cnt_ref), (core_in, core_ref), (pw_in, pw_ref),
        ))
    ]
    for c in loads:
        c.start()
    barrier = pltpu.get_barrier_semaphore()
    partners = (
        [xdev] + [fdev(d) for d in range(1, 4)]
        + [ydev(d) for d in range(1, ny)] + [zdev(d) for d in range(1, nz)]
    )
    for dev in partners:
        pl.semaphore_signal(barrier, inc=1, device_id=dev, device_id_type=pl.DeviceIdType.MESH)
    pl.semaphore_wait(barrier, len(partners))

    xcopy = remote(codes_in, xbuf.at[xh], xsem, 0, xdev)
    xcopy.start()
    loads[0].wait()
    xcopy.wait()
    g1 = []
    for d in range(1, ny):
        g1.append(remote(xbuf.at[:, :, pl.ds(0, half)], ga.at[:, y], g1sem, d, ydev(d)))
    for d in range(1, nz):
        g1.append(remote(xbuf.at[:, :, pl.ds(half, half)], gb.at[z], g1sem, ny + d, zdev(d)))
    for c in g1:
        c.start()
    for j in range(nx):
        ga[j, y] = xbuf[j, :, 0:half]
        gb[z, j] = xbuf[j, :, half:ncode]

    for c in loads[1:]:
        c.wait()
    mk[:, nvis:, :] = jnp.zeros((npat, VP - nvis, ncode), BF16)

    def mask_patient(k, carry):
        for t in range(ntile):
            cols = slice(t * tile, (t + 1) * tile)
            v = vis[k, :, cols]
            mk[k, 0:nvis, cols] = jnp.where(pat_ref[k, t] > 0, v, jnp.zeros_like(v))
        return carry

    lax.fori_loop(0, npat, mask_patient, 0)

    axes = ((ca, z, nz, zdev), (cb, y, ny, ydev))
    streams = [(way, c) for way in (0, 1) for c in (0, 1)]
    pending = list(g1)
    live = {}

    def hops(n, way, c):
        return n // 2 if way == c else n - 1 - n // 2

    def ring_copy(a, way, c, t):
        buf, me, n, dev = axes[a]
        sign = 1 - 2 * way
        part = buf.at[(me - sign * t + n) % n, c]
        return remote(part, part, ringsem, ((a * 2 + way) * 2 + c) * 4 + t, dev(sign))

    def start_rings(a):
        for way, c in streams:
            if hops(axes[a][2], way, c):
                live[a, way, c] = ring_copy(a, way, c, 0)
                live[a, way, c].start()

    for c in g1[: ny - 1]:
        c.wait_recv()
    for s in range(nx * ny):
        rel[2 * s : 2 * s + 2, :] = ga[s // ny, s % ny].astype(F32)
    ca[z] = rel[0 : 2 * nx * ny, :].astype(BF16).reshape(ca.shape[1:])
    start_rings(0)
    for c in g1[ny - 1 :]:
        c.wait_recv()
    for s in range(nz * nx):
        rel[2 * s : 2 * s + 2, :] = gb[s // nx, s % nx].astype(F32)
    cb[y] = rel[0 : 2 * nz * nx, :].astype(BF16).reshape(cb.shape[1:])
    start_rings(1)
    for t in range(1, max(nz, ny) // 2 + 1):
        for a in (0, 1):
            for way, c in streams:
                steps = hops(axes[a][2], way, c)
                if t > steps:
                    continue
                live[a, way, c].wait_recv()
                pending.append(live[a, way, c])
                if t < steps:
                    live[a, way, c] = ring_copy(a, way, c, t)
                    live[a, way, c].start()

    blk = 2 * nz * nx

    def natural(rp):
        yy, rest = rp // blk, rp % blk
        zx, i = rest // 2, rest % 2
        return (zx // nx) * (2 * nx * ny) + (zx % nx) * (2 * ny) + yy * 2 + i

    rows = lax.broadcasted_iota(jnp.int32, (rank, rank), 0)
    cols = lax.broadcasted_iota(jnp.int32, (rank, rank), 1)
    to_nat = jnp.where(rows == natural(cols), 1.0, 0.0).astype(BF16)
    to_b = jnp.where(natural(rows) == cols, 1.0, 0.0).astype(BF16)

    cbn = mm(to_nat, cb[...].reshape(rank, half)).astype(BF16)
    flat = npat * VP
    proj = lax.dot_general(
        mk[:, :, 0:half].reshape(flat, half), ca[...].reshape(rank, half), NT,
        preferred_element_type=F32,
    ) + lax.dot_general(
        mk[:, :, half:ncode].reshape(flat, half), cbn, NT, preferred_element_type=F32
    )
    own = flat // 4
    projf[...] = proj.reshape(2, 2, own, rank)

    fa = remote(projf.at[:, 1 - core], ra, featsem, 0, at(z, xh, y, xlo * 2 + 1 - core))
    fa.start()
    fa.wait()
    sb[...] = projf[1 - xlo, core] + ra[1 - xlo]
    fb = remote(sb, rb, featsem, 1, at(z, xh, y, (1 - xlo) * 2 + core))
    fb.start()
    mine = projf[xlo, core] + ra[xlo]
    fb.wait()
    projected = mine + rb[...]

    np_own = npat // 4
    rowi = lax.broadcasted_iota(jnp.int32, (own, rank), 0)
    limit = jnp.full((own, rank), cnt_ref[feat * np_own], jnp.int32)
    weights = jnp.broadcast_to(pw_ref[pl.ds(feat * np_own, 1), :], (own, rank))
    for p in range(1, np_own):
        here = rowi >= p * VP
        limit = jnp.where(here, cnt_ref[feat * np_own + p] + p * VP, limit)
        weights = jnp.where(here, pw_ref[pl.ds(feat * np_own + p, 1), :], weights)
    projected = jnp.where(rowi < limit, projected, 0.0)
    hi, lo = split2(projected * weights)
    core_w = core_ref[...]
    both = lax.dot_general(
        jnp.concatenate([hi, lo], axis=0), core_w, NT, preferred_element_type=F32
    )
    target = both[0:own] + both[own:]
    hi, lo = split2(target)
    gram = lax.dot_general(
        jnp.concatenate([hi, lo, hi], axis=1), jnp.concatenate([hi, hi, lo], axis=1), NT,
        preferred_element_type=F32,
    )
    both = mm(jnp.concatenate([hi, lo], axis=0), core_w)
    base = both[0:own] + both[own:]
    gi = lax.broadcasted_iota(jnp.int32, (own, own), 0)
    gj = lax.broadcasted_iota(jnp.int32, (own, own), 1)
    square = jnp.sum(target * target, axis=1, keepdims=True)
    scale = jnp.zeros((own, 1), F32)
    pi = lax.broadcasted_iota(jnp.int32, (own, 1), 0) // VP
    for p in range(np_own):
        total = jnp.sum(square[p * VP : (p + 1) * VP], axis=0, keepdims=True)
        scale = jnp.where(pi == p, lax.rsqrt(total + 1e-06), scale)
    gram = jnp.where(gi // VP == gj // VP, gram * (scale * scale), 0.0)
    eye = jnp.where(gi == gj, 1.0, 0.0)
    base = base * scale

    def grow(g, right):
        half_step = 1.5 * g - 0.5 * mm(left3(g), right)
        return 1.5 * half_step - 0.5 * mm(left3(half_step), right)

    poly = 1.5 * eye - 0.5 * gram
    gram = grow(gram, right3(gram))

    def ns_step(i, carry):
        poly, gram = carry
        right = right3(gram)
        return (1.5 * poly - 0.5 * mm(left3(poly), right), grow(gram, right))

    poly, gram = lax.fori_loop(0, NS_STEPS - 2, ns_step, (poly, gram))
    poly = 1.5 * poly - 0.5 * mm(left3(poly), right3(gram))
    rotated = mm(left3(poly), right3(base))
    prod = rotated * projected
    for p in range(np_own):
        prow[feat, p : p + 1, :] = jnp.sum(prod[p * VP : (p + 1) * VP], axis=0, keepdims=True)
    wbuf[feat] = (rotated * weights).T.astype(BF16)
    wcopies = []
    for d in range(1, 4):
        wcopies.append(remote(wbuf.at[feat], wbuf.at[feat], wsem, d, fdev(d)))
        wcopies.append(remote(prow.at[feat], prow.at[feat], psem, d, fdev(d)))
    for c in wcopies:
        c.start()
    for c in wcopies:
        c.wait_recv()
    pending += wcopies

    for f in range(4):
        wt[:, f * own : (f + 1) * own] = wbuf[f]
        out_pat[f * np_own : (f + 1) * np_own, :] = prow[f]
    wt_b = mm(to_b, wt[...]).astype(BF16)
    terms = (ta, tb)
    live = {}

    def arrived(a, way, c, t):
        live[a, way, c].wait_recv()
        return dequant(qr[a, way, c, t])

    def send_sum(a, way, c, t):
        _, me, n, dev = axes[a]
        sign = 1 - 2 * way
        v = terms[a][(me + sign * (hops(n, way, c) - t) + n) % n, c]
        if t:
            v = v + arrived(a, way, c, t - 1)
        qs[a, way, c, t] = quant(v)
        copy = remote(
            qs.at[a, way, c, t], qr.at[a, way, c, t], rsem,
            ((a * 2 + way) * 2 + c) * 4 + t, dev(sign),
        )
        copy.start()
        live[a, way, c] = copy
        pending.append(copy)

    ta[...] = mm(wt[...], mk[:, :, 0:half].reshape(flat, half)).reshape(ta.shape)
    for way, c in streams:
        if hops(nz, way, c):
            send_sum(0, way, c, 0)
    tb[...] = mm(wt_b, mk[:, :, half:ncode].reshape(flat, half)).reshape(tb.shape)
    for way, c in streams:
        if hops(ny, way, c):
            send_sum(1, way, c, 0)
    for t in range(1, max(nz, ny) // 2):
        for a in (0, 1):
            for way, c in streams:
                if t < hops(axes[a][2], way, c):
                    send_sum(a, way, c, t)

    def ring_total(a):
        _, me, n, _ = axes[a]
        out = []
        for c in (0, 1):
            v = terms[a][me, c]
            for way in (0, 1):
                steps = hops(n, way, c)
                if steps:
                    v = v + arrived(a, way, c, steps - 1)
            out.append(v)
        return jnp.concatenate(out, axis=0)

    rel[0 : 2 * nx * ny, :] = ring_total(0)
    for s in range(nx * ny):
        s2a[s % ny, s // ny] = rel[2 * s : 2 * s + 2, :]
    g2 = []
    for d in range(1, ny):
        to = (y + d) % ny
        g2.append(remote(s2a.at[to], r2a.at[y], g2sem, d, ydev(d)))
    for c in g2:
        c.start()
    rel[0 : 2 * nz * nx, :] = ring_total(1)
    for s in range(nz * nx):
        s2b[s // nx, s % nx] = rel[2 * s : 2 * s + 2, :]
    g3 = []
    for d in range(1, nz):
        to = (z + d) % nz
        g3.append(remote(s2b.at[to], r2b.at[z], g2sem, ny + d, zdev(d)))
    for c in g3:
        c.start()
    pending += g2 + g3
    for c in g2:
        c.wait_recv()
    suma = s2a[y]
    for d in range(1, ny):
        suma = suma + r2a[(y + d) % ny]
    for c in g3:
        c.wait_recv()
    sumb = s2b[z]
    for d in range(1, nz):
        sumb = sumb + r2b[(z + d) % nz]
    xs[:, :, 0:half] = suma
    xs[:, :, half:ncode] = sumb
    xf = remote(xs.at[1 - xh], xr, xfsem, 0, xdev)
    xf.start()
    xf.wait()
    out_codes[...] = xs[xh] + xr[...]
    for c in pending:
        c.wait_send()


def per_device(visits, tile_pattern, counts, codes_t, core, patient_weights, dims):
    nz, nx, ny = dims
    npat, nvis, ncode = visits.shape
    rank = core.shape[0]
    half = ncode // 2
    rows_a, rows_b = 2 * nx * ny, 2 * nz * nx
    flat = npat * VP
    own = flat // 4
    dma = pltpu.SemaphoreType.DMA
    vmem = pl.BlockSpec(memory_space=pltpu.VMEM)
    scratch = [
        pltpu.VMEM((npat, nvis, ncode), BF16),
        pltpu.SMEM(tile_pattern.shape, jnp.int32),
        pltpu.SMEM(counts.shape, jnp.int32),
        pltpu.VMEM(core.shape, BF16),
        pltpu.VMEM(patient_weights.shape, F32),
        pltpu.VMEM((npat, VP, ncode), BF16),
        pltpu.VMEM((nx, 2, ncode), BF16),
        pltpu.VMEM((nx, ny, 2, half), BF16),
        pltpu.VMEM((nz, nx, 2, half), BF16),
        pltpu.VMEM((max(rows_a, rows_b), half), F32),
        pltpu.VMEM((nz, 2, rows_a // 2, half), BF16),
        pltpu.VMEM((ny, 2, rows_b // 2, half), BF16),
        pltpu.VMEM((2, 2, own, rank), F32),
        pltpu.VMEM((2, own, rank), F32),
        pltpu.VMEM((own, rank), F32),
        pltpu.VMEM((own, rank), F32),
        pltpu.VMEM((4, rank, own), BF16),
        pltpu.VMEM((4, npat // 4, rank), F32),
        pltpu.VMEM((rank, flat), BF16),
        pltpu.VMEM((nz, 2, rows_a // 2, half), F32),
        pltpu.VMEM((ny, 2, rows_b // 2, half), F32),
        pltpu.VMEM((2, 2, 2, 4, rows_a // 2, half + 128), I16),
        pltpu.VMEM((2, 2, 2, 4, rows_a // 2, half + 128), I16),
        pltpu.VMEM((ny, nx, 2, half), F32),
        pltpu.VMEM((ny, nx, 2, half), F32),
        pltpu.VMEM((nz, nx, 2, half), F32),
        pltpu.VMEM((nz, nx, 2, half), F32),
        pltpu.VMEM((nx, 2, ncode), F32),
        pltpu.VMEM((2, ncode), F32),
        dma((6,)),
        dma((2, 1)),
        dma((2, ny + nz)),
        dma((2, 32)),
        dma((2, 2)),
        dma((2, 4)),
        dma((2, 4)),
        dma((2, 32)),
        dma((2, ny + nz)),
        dma((2, 1)),
    ]
    return pl.pallas_call(
        functools.partial(kernel, dims),
        out_shape=(
            jax.ShapeDtypeStruct(codes_t.shape, F32),
            jax.ShapeDtypeStruct(patient_weights.shape, F32),
        ),
        in_specs=[pl.BlockSpec(memory_space=pltpu.HBM)] * 6,
        out_specs=(vmem, vmem),
        scratch_shapes=scratch,
        compiler_params=pltpu.CompilerParams(
            collective_id=0, has_side_effects=True, vmem_limit_bytes=60 * 1024 * 1024
        ),
        name="sweep",
    )(visits, tile_pattern, counts, codes_t, core, patient_weights)


def build(mesh, dims):
    return jax.shard_map(
        functools.partial(per_device, dims=dims),
        mesh=mesh,
        in_specs=(
            P("subj", None, "feat"),
            P("subj", "feat"),
            P("subj"),
            P("subj", "feat"),
            P(),
            P("subj", None),
        ),
        out_specs=(P("subj", "feat"), P("subj", None)),
        check_vma=False,
    )


def solution(mesh):
    return build(mesh, (NZ, NX, NY))
```

```python
import functools

import jax
import jax.numpy as jnp
from jax import lax
from jax.experimental import pallas as pl
from jax.experimental.pallas import tpu as pltpu
from jax.sharding import PartitionSpec as P

NS_STEPS = 8
NZ, NX, NY = 8, 2, 8
VP = 64
QMAX = 32000.0
F32 = jnp.float32
BF16 = jnp.bfloat16
I16 = jnp.int16
NT = (((1,), (1,)), ((), ()))


def split2(x):
    hi = x.astype(BF16)
    lo = (x - hi.astype(F32)).astype(BF16)
    return hi, lo


def left3(x):
    hi, lo = split2(x)
    return jnp.concatenate([hi, lo, hi], axis=1)


def right3(x):
    hi, lo = split2(x)
    return jnp.concatenate([hi, hi, lo], axis=0)


def mm(a, b):
    return jnp.dot(a, b, preferred_element_type=F32)


def tree(n):
    return {
        8: ((2, -2, 1, -1), ((2, 1, None), (-2, -1, None), (2, 2, 0), (-2, -2, 1))),
        4: ((1, -1), ((1, 1, 0), (-1, -1, 1))),
        2: ((1,), ()),
        1: ((), ()),
    }[n]


def encode(parts):
    top = jnp.abs(parts[0])
    for part in parts[1:]:
        top = jnp.maximum(top, jnp.abs(part))
    exponent = jnp.floor(jnp.log2(jnp.maximum(top, 1e-30))) + 1.0
    scale = jnp.exp2(-exponent) * QMAX
    return [jnp.round(part * scale) for part in parts] + [exponent]


def decode(parts):
    scale = jnp.exp2(parts[-1]) * (1.0 / QMAX)
    return [part * scale for part in parts[:-1]]


def to_i16(v):
    return v.astype(jnp.int32).astype(I16)


def from_i16(q):
    return q.astype(jnp.int32).astype(F32)


def tiles(v):
    return [v[..., c : c + 128] for c in range(0, v.shape[-1], 128)]


def codes_of(v):
    return jnp.concatenate(encode(tiles(v)), axis=-1)


def values_of(q):
    return jnp.concatenate(decode(tiles(from_i16(q))), axis=-1)


def patient_codes(v, nvis):
    out = []
    for p in range(0, v.shape[0], VP):
        out += encode([v[p + r : p + r + 8] for r in range(0, nvis, 8)])
    return to_i16(jnp.concatenate(out, axis=0))


def patient_values(q, nvis):
    v = from_i16(q)
    out = []
    for p in range(0, v.shape[0], VP):
        out += decode([v[p + r : p + r + 8] for r in range(0, nvis + 8, 8)])
        out.append(jnp.zeros((8, v.shape[1]), F32))
    return jnp.concatenate(out, axis=0)


def kernel(
    dims,
    visits_in, pat_in, cnt_in, codes_in, core_in, pw_in,
    out_codes, out_pat,
    vis, pat_ref, cnt_ref, core_ref, pw_ref, mk, xbuf, ga, gb, rel, ca, cb, projf, ra, rb, sb, wbuf, prow, wt, ta, tb,
    qs_a, qr_a, qs_b, qr_b, s2a, r2a, s2b, r2b, xs, xr,
    lsem, xsem, g1sem, ringsem, featsem, wsem, psem, rsem, g2sem, xfsem,
):
    nz, nx, ny = dims
    npat, nvis, ncode = visits_in.shape
    rank = core_ref.shape[0]
    half = ncode // 2
    ntile = pat_ref.shape[1]
    tile = ncode // ntile
    subj = lax.axis_index("subj")
    feat = lax.axis_index("feat")
    z = subj // (nx * ny)
    xh = (subj // ny) % nx
    y = subj % ny
    xlo, core = feat // 2, feat % 2

    def at(zz, xx, yy, ff):
        return {"subj": (zz * nx + xx) * ny + yy, "feat": ff}

    def zdev(d):
        return at((z + d + nz) % nz, xh, y, feat)

    def ydev(d):
        return at(z, xh, (y + d + ny) % ny, feat)

    xdev = at(z, 1 - xh, y, feat)

    def fdev(d):
        return at(z, xh, y, (feat + d) % 4)

    def remote(src, dst, sems, i, dev):
        return pltpu.make_async_remote_copy(
            src_ref=src, dst_ref=dst, send_sem=sems.at[0, i], recv_sem=sems.at[1, i],
            device_id=dev, device_id_type=pl.DeviceIdType.MESH,
        )

    loads = [
        pltpu.make_async_copy(src, dst, lsem.at[i])
        for i, (src, dst) in enumerate((
            (codes_in, xbuf.at[xh]), (pat_in, pat_ref), (visits_in, vis),
            (cnt_in, cnt_ref), (core_in, core_ref), (pw_in, pw_ref),
        ))
    ]
    for c in loads:
        c.start()
    barrier = pltpu.get_barrier_semaphore()
    partners = (
        [xdev] + [fdev(d) for d in range(1, 4)]
        + [ydev(d) for d in range(1, ny)] + [zdev(d) for d in range(1, nz)]
    )
    for dev in partners:
        pl.semaphore_signal(barrier, inc=1, device_id=dev, device_id_type=pl.DeviceIdType.MESH)
    pl.semaphore_wait(barrier, len(partners))

    xcopy = remote(codes_in, xbuf.at[xh], xsem, 0, xdev)
    xcopy.start()
    loads[0].wait()
    xcopy.wait()
    g1 = []
    for d in range(1, ny):
        g1.append(remote(xbuf.at[:, :, pl.ds(0, half)], ga.at[:, y], g1sem, d, ydev(d)))
    for d in range(1, nz):
        g1.append(remote(xbuf.at[:, :, pl.ds(half, half)], gb.at[z], g1sem, ny + d, zdev(d)))
    for c in g1:
        c.start()
    for j in range(nx):
        ga[j, y] = xbuf[j, :, 0:half]
        gb[z, j] = xbuf[j, :, half:ncode]

    for c in loads[1:]:
        c.wait()
    mk[:, nvis:, :] = jnp.zeros((npat, VP - nvis, ncode), BF16)

    def mask_patient(k, carry):
        for t in range(ntile):
            cols = slice(t * tile, (t + 1) * tile)
            v = vis[k, :, cols]
            mk[k, 0:nvis, cols] = jnp.where(pat_ref[k, t] > 0, v, jnp.zeros_like(v))
        return carry

    lax.fori_loop(0, npat, mask_patient, 0)

    axes = ((ca, z, nz, zdev), (cb, y, ny, ydev))
    pending = list(g1)
    live = {}

    def ring_copy(a, back, step, part, e):
        buf, me, n, dev = axes[a]
        block = buf.at[(me - back + n) % n]
        block = block if part is None else block.at[part]
        copy = remote(block, block, ringsem, a * 8 + e, dev(step))
        copy.start()
        pending.append(copy)
        return copy

    def start_rings(a):
        for e, k in enumerate(tree(axes[a][2])[0]):
            live[a, k] = ring_copy(a, 0, k, None, e)

    for c in g1[: ny - 1]:
        c.wait_recv()
    for s in range(nx * ny):
        rel[2 * s : 2 * s + 2, 0:half] = ga[s // ny, s % ny].astype(F32)
    ca[z] = rel[0 : 2 * nx * ny, 0:half].astype(BF16).reshape(ca.shape[1:])
    start_rings(0)
    for c in g1[ny - 1 :]:
        c.wait_recv()
    for s in range(nz * nx):
        rel[2 * s : 2 * s + 2, 0:half] = gb[s // nx, s % nx].astype(F32)
    cb[y] = rel[0 : 2 * nz * nx, 0:half].astype(BF16).reshape(cb.shape[1:])
    start_rings(1)
    passed = set()
    for e in range(4):
        for a in (0, 1):
            first, later = tree(axes[a][2])
            if e < len(later):
                k, step, part = later[e]
                if (a, k) not in passed:
                    live[a, k].wait_recv()
                    passed.add((a, k))
                live[a, k, step] = ring_copy(a, k, step, part, len(first) + e)
    for key in live:
        if key not in passed:
            live[key].wait_recv()

    blk = 2 * nz * nx

    def natural(rp):
        yy, rest = rp // blk, rp % blk
        zx, i = rest // 2, rest % 2
        return (zx // nx) * (2 * nx * ny) + (zx % nx) * (2 * ny) + yy * 2 + i

    rows = lax.broadcasted_iota(jnp.int32, (rank, rank), 0)
    cols = lax.broadcasted_iota(jnp.int32, (rank, rank), 1)
    to_nat = jnp.where(rows == natural(cols), 1.0, 0.0).astype(BF16)
    to_b = jnp.where(natural(rows) == cols, 1.0, 0.0).astype(BF16)

    cbn = mm(to_nat, cb[...].reshape(rank, half)).astype(BF16)
    flat = npat * VP
    proj = lax.dot_general(
        mk[:, :, 0:half].reshape(flat, half), ca[...].reshape(rank, half), NT,
        preferred_element_type=F32,
    ) + lax.dot_general(
        mk[:, :, half:ncode].reshape(flat, half), cbn, NT, preferred_element_type=F32
    )
    own = flat // 4
    projf[...] = proj.reshape(2, 2, own, rank)

    fa = remote(projf.at[:, 1 - core], ra, featsem, 0, at(z, xh, y, xlo * 2 + 1 - core))
    fa.start()
    fa.wait()
    sb[...] = patient_codes(projf[1 - xlo, core] + ra[1 - xlo], nvis)
    fb = remote(sb, rb, featsem, 1, at(z, xh, y, (1 - xlo) * 2 + core))
    fb.start()
    mine = projf[xlo, core] + ra[xlo]
    fb.wait()
    projected = mine + patient_values(rb[...], nvis)

    np_own = npat // 4
    rowi = lax.broadcasted_iota(jnp.int32, (own, rank), 0)
    limit = jnp.full((own, rank), cnt_ref[feat * np_own], jnp.int32)
    weights = jnp.broadcast_to(pw_ref[pl.ds(feat * np_own, 1), :], (own, rank))
    for p in range(1, np_own):
        here = rowi >= p * VP
        limit = jnp.where(here, cnt_ref[feat * np_own + p] + p * VP, limit)
        weights = jnp.where(here, pw_ref[pl.ds(feat * np_own + p, 1), :], weights)
    projected = jnp.where(rowi < limit, projected, 0.0)
    hi, lo = split2(projected * weights)
    core_w = core_ref[...]
    both = lax.dot_general(
        jnp.concatenate([hi, lo], axis=0), core_w, NT, preferred_element_type=F32
    )
    target = both[0:own] + both[own:]
    hi, lo = split2(target)
    gram = lax.dot_general(
        jnp.concatenate([hi, lo, hi], axis=1), jnp.concatenate([hi, hi, lo], axis=1), NT,
        preferred_element_type=F32,
    )
    both = mm(jnp.concatenate([hi, lo], axis=0), core_w)
    base = both[0:own] + both[own:]
    gi = lax.broadcasted_iota(jnp.int32, (own, own), 0)
    gj = lax.broadcasted_iota(jnp.int32, (own, own), 1)
    square = jnp.sum(target * target, axis=1, keepdims=True)
    scale = jnp.zeros((own, 1), F32)
    pi = lax.broadcasted_iota(jnp.int32, (own, 1), 0) // VP
    for p in range(np_own):
        total = jnp.sum(square[p * VP : (p + 1) * VP], axis=0, keepdims=True)
        scale = jnp.where(pi == p, lax.rsqrt(total + 1e-06), scale)
    gram = jnp.where(gi // VP == gj // VP, gram * (scale * scale), 0.0)
    eye = jnp.where(gi == gj, 1.0, 0.0)
    base = base * scale

    def grow(g, right):
        half_step = 1.5 * g - 0.5 * mm(left3(g), right)
        return 1.5 * half_step - 0.5 * mm(left3(half_step), right)

    poly = 1.5 * eye - 0.5 * gram
    gram = grow(gram, right3(gram))

    def ns_step(i, carry):
        poly, gram = carry
        right = right3(gram)
        return (1.5 * poly - 0.5 * mm(left3(poly), right), grow(gram, right))

    poly, gram = lax.fori_loop(0, NS_STEPS - 2, ns_step, (poly, gram))
    poly = 1.5 * poly - 0.5 * mm(left3(poly), right3(gram))
    rotated = mm(left3(poly), right3(base))
    prod = rotated * projected
    for p in range(np_own):
        prow[feat, p : p + 1, :] = jnp.sum(prod[p * VP : (p + 1) * VP], axis=0, keepdims=True)
    wbuf[feat] = (rotated * weights).T.astype(BF16)
    sib = at(z, xh, y, xlo * 2 + 1 - core)
    over = at(z, xh, y, (1 - xlo) * 2 + core)
    across = remote(wbuf.at[feat], wbuf.at[feat], wsem, 0, over)
    across.start()
    beside = remote(wbuf.at[feat], wbuf.at[feat], wsem, 1, sib)
    beside.start()
    pcopies = [remote(prow.at[feat], prow.at[feat], psem, d, fdev(d)) for d in range(1, 4)]
    for c in pcopies:
        c.start()
    across.wait_recv()
    passed_on = remote(wbuf.at[(feat + 2) % 4], wbuf.at[(feat + 2) % 4], wsem, 2, sib)
    passed_on.start()
    beside.wait_recv()
    passed_on.wait_recv()
    pending += [across, beside, passed_on] + pcopies
    for f in range(4):
        wt[:, f * own : (f + 1) * own] = wbuf[f]
    wt_b = mm(to_b, wt[...]).astype(BF16)
    terms = (ta, tb)
    live = {}

    def send_sums(a, e, dest, step, parts, extra):
        qs, qr = (qs_a, qr_a) if a == 0 else (qs_b, qr_b)
        for c in parts:
            v = terms[a][dest, c]
            for other in extra:
                if c in other[1]:
                    v = v + values_of(qr[other[0], c])
            qs[e, c] = to_i16(codes_of(v))
        src, dst = qs.at[e], qr.at[e]
        if len(parts) == 1:
            src, dst = src.at[parts[0]], dst.at[parts[0]]
        copy = remote(src, dst, rsem, a * 8 + e, axes[a][3](-step))
        copy.start()
        live[a, e] = copy
        pending.append(copy)

    def leaves(a):
        _, me, n, _ = axes[a]
        first, later = tree(n)
        for e, (k, step, part) in enumerate(later):
            parts = (0, 1) if part is None else (part,)
            send_sums(a, len(first) + e, (me - k - step + n) % n, step, parts, ())

    def joined(a, k):
        first, later = tree(axes[a][2])
        return [
            (len(first) + e, (0, 1) if part is None else (part,))
            for e, (kk, _, part) in enumerate(later) if kk == k
        ]

    def inner(a, ready):
        _, me, n, _ = axes[a]
        for e, k in enumerate(tree(n)[0]):
            extra = joined(a, k)
            if ready != bool(extra):
                for other in extra:
                    live[a, other[0]].wait_recv()
                send_sums(a, e, (me - k + n) % n, k, (0, 1), extra)

    ta[...] = mm(wt[...], mk[:, :, 0:half].reshape(flat, half)).reshape(ta.shape)
    leaves(0)
    tb[...] = mm(wt_b, mk[:, :, half:ncode].reshape(flat, half)).reshape(tb.shape)
    leaves(1)
    for a in (0, 1):
        inner(a, True)
    for a in (0, 1):
        inner(a, False)

    def ring_total(a):
        _, me, n, _ = axes[a]
        qr = qr_a if a == 0 else qr_b
        first = tree(n)[0]
        for e in range(len(first)):
            live[a, e].wait_recv()
        rows = terms[a].shape[2]
        for c in (0, 1):
            v = terms[a][me, c]
            for e in range(len(first)):
                v = v + values_of(qr[e, c])
            rel[c * rows : (c + 1) * rows, :] = codes_of(v)

    ring_total(0)
    for s in range(nx * ny):
        s2a[s % ny, s // ny] = to_i16(rel[2 * s : 2 * s + 2, :])
    g2 = []
    for d in range(1, ny):
        g2.append(remote(s2a.at[(y + d) % ny], r2a.at[y], g2sem, d, ydev(d)))
        g2[-1].start()
    ring_total(1)
    for s in range(nz * nx):
        s2b[s // nx, s % nx] = to_i16(rel[2 * s : 2 * s + 2, :])
    g3 = []
    for d in range(1, nz):
        g3.append(remote(s2b.at[(z + d) % nz], r2b.at[z], g2sem, ny + d, zdev(d)))
        g3[-1].start()
    pending += g2 + g3
    for c in pcopies:
        c.wait_recv()
    for f in range(4):
        out_pat[f * np_own : (f + 1) * np_own, :] = prow[f]
    for c in g2:
        c.wait_recv()
    suma = values_of(s2a[y])
    for d in range(1, ny):
        suma = suma + values_of(r2a[(y + d) % ny])
    for c in g3:
        c.wait_recv()
    sumb = values_of(s2b[z])
    for d in range(1, nz):
        sumb = sumb + values_of(r2b[(z + d) % nz])
    xs[:, :, 0:half] = suma
    xs[:, :, half:ncode] = sumb
    xf = remote(xs.at[1 - xh], xr, xfsem, 0, xdev)
    xf.start()
    xf.wait()
    out_codes[...] = xs[xh] + xr[...]
    for c in pending:
        c.wait_send()


def per_device(visits, tile_pattern, counts, codes_t, core, patient_weights, dims):
    nz, nx, ny = dims
    npat, nvis, ncode = visits.shape
    rank = core.shape[0]
    half = ncode // 2
    rows_a, rows_b = 2 * nx * ny, 2 * nz * nx
    flat = npat * VP
    own = flat // 4
    dma = pltpu.SemaphoreType.DMA
    vmem = pl.BlockSpec(memory_space=pltpu.VMEM)
    scratch = [
        pltpu.VMEM((npat, nvis, ncode), BF16),
        pltpu.SMEM(tile_pattern.shape, jnp.int32),
        pltpu.SMEM(counts.shape, jnp.int32),
        pltpu.VMEM(core.shape, BF16),
        pltpu.VMEM(patient_weights.shape, F32),
        pltpu.VMEM((npat, VP, ncode), BF16),
        pltpu.VMEM((nx, 2, ncode), BF16),
        pltpu.VMEM((nx, ny, 2, half), BF16),
        pltpu.VMEM((nz, nx, 2, half), BF16),
        pltpu.VMEM((max(rows_a, rows_b), half + 128), F32),
        pltpu.VMEM((nz, 2, rows_a // 2, half), BF16),
        pltpu.VMEM((ny, 2, rows_b // 2, half), BF16),
        pltpu.VMEM((2, 2, own, rank), F32),
        pltpu.VMEM((2, own, rank), F32),
        pltpu.VMEM((own, rank), I16),
        pltpu.VMEM((own, rank), I16),
        pltpu.VMEM((4, rank, own), BF16),
        pltpu.VMEM((4, npat // 4, rank), F32),
        pltpu.VMEM((rank, flat), BF16),
        pltpu.VMEM((nz, 2, rows_a // 2, half), F32),
        pltpu.VMEM((ny, 2, rows_b // 2, half), F32),
        pltpu.VMEM((8, 2, rows_a // 2, half + 128), I16),
        pltpu.VMEM((8, 2, rows_a // 2, half + 128), I16),
        pltpu.VMEM((8, 2, rows_b // 2, half + 128), I16),
        pltpu.VMEM((8, 2, rows_b // 2, half + 128), I16),
        pltpu.VMEM((ny, nx, 2, half + 128), I16),
        pltpu.VMEM((ny, nx, 2, half + 128), I16),
        pltpu.VMEM((nz, nx, 2, half + 128), I16),
        pltpu.VMEM((nz, nx, 2, half + 128), I16),
        pltpu.VMEM((nx, 2, ncode), F32),
        pltpu.VMEM((2, ncode), F32),
        dma((6,)),
        dma((2, 1)),
        dma((2, ny + nz)),
        dma((2, 32)),
        dma((2, 2)),
        dma((2, 4)),
        dma((2, 4)),
        dma((2, 32)),
        dma((2, ny + nz)),
        dma((2, 1)),
    ]
    return pl.pallas_call(
        functools.partial(kernel, dims),
        out_shape=(
            jax.ShapeDtypeStruct(codes_t.shape, F32),
            jax.ShapeDtypeStruct(patient_weights.shape, F32),
        ),
        in_specs=[pl.BlockSpec(memory_space=pltpu.HBM)] * 6,
        out_specs=(vmem, vmem),
        scratch_shapes=scratch,
        compiler_params=pltpu.CompilerParams(
            collective_id=0, has_side_effects=True, vmem_limit_bytes=60 * 1024 * 1024
        ),
        name="sweep",
    )(visits, tile_pattern, counts, codes_t, core, patient_weights)


def build(mesh, dims):
    return jax.shard_map(
        functools.partial(per_device, dims=dims),
        mesh=mesh,
        in_specs=(
            P("subj", None, "feat"),
            P("subj", "feat"),
            P("subj"),
            P("subj", "feat"),
            P(),
            P("subj", None),
        ),
        out_specs=(P("subj", "feat"), P("subj", None)),
        check_vma=False,
    )


def solution(mesh):
    return build(mesh, (NZ, NX, NY))
```

```python
import functools

import jax
import jax.numpy as jnp
from jax import lax
from jax.experimental import pallas as pl
from jax.experimental.pallas import tpu as pltpu
from jax.sharding import PartitionSpec as P

NS_STEPS = 8
NZ, NX, NY = 8, 2, 8
VP = 64
QMAX = 32000.0
F32 = jnp.float32
BF16 = jnp.bfloat16
I16 = jnp.int16
NT = (((1,), (1,)), ((), ()))


def split2(x):
    hi = x.astype(BF16)
    lo = (x - hi.astype(F32)).astype(BF16)
    return hi, lo


def left3(x):
    hi, lo = split2(x)
    return jnp.concatenate([hi, lo, hi], axis=1)


def right3(x):
    hi, lo = split2(x)
    return jnp.concatenate([hi, hi, lo], axis=0)


def mm(a, b):
    return jnp.dot(a, b, preferred_element_type=F32)


def tree(n, far):
    return {
        8: ((2, -2, 1, -1), ((2, 1), (-2, -1), (2 * far, 2 * far))),
        4: ((1, -1), ((far, far),)),
        2: ((1,), ()),
        1: ((), ()),
    }[n]


def encode(parts):
    top = jnp.abs(parts[0])
    for part in parts[1:]:
        top = jnp.maximum(top, jnp.abs(part))
    exponent = jnp.floor(jnp.log2(jnp.maximum(top, 1e-30))) + 1.0
    scale = jnp.exp2(-exponent) * QMAX
    return [jnp.round(part * scale) for part in parts] + [exponent]


def decode(parts):
    scale = jnp.exp2(parts[-1]) * (1.0 / QMAX)
    return [part * scale for part in parts[:-1]]


def to_i16(v):
    return v.astype(jnp.int32).astype(I16)


def from_i16(q):
    return q.astype(jnp.int32).astype(F32)


def tiles(v):
    return [v[..., c : c + 128] for c in range(0, v.shape[-1], 128)]


def codes_of(v):
    return jnp.concatenate(encode(tiles(v)), axis=-1)


def values_of(q):
    return jnp.concatenate(decode(tiles(from_i16(q))), axis=-1)


def patient_codes(v, nvis):
    out = []
    for p in range(0, v.shape[0], VP):
        out += encode([v[p + r : p + r + 8] for r in range(0, nvis, 8)])
    return to_i16(jnp.concatenate(out, axis=0))


def patient_values(q, nvis):
    v = from_i16(q)
    out = []
    for p in range(0, v.shape[0], VP):
        out += decode([v[p + r : p + r + 8] for r in range(0, nvis + 8, 8)])
        out.append(jnp.zeros((8, v.shape[1]), F32))
    return jnp.concatenate(out, axis=0)


def kernel(
    dims,
    visits_in, pat_in, cnt_in, codes_in, core_in, pw_in,
    out_codes, out_pat,
    vis, pat_ref, cnt_ref, core_ref, pw_ref, mk, piece, ga, gb, rel, ca, cb, projf, ra, rb, sb, wbuf, prow, wt, to_nat, to_b, ta, tb,
    qs_a, qr_a, qs_b, qr_b, s2a, r2a, s2b, r2b, xs_a, xr_a, xs_b, xr_b,
    lsem, xsem, g1sem, ringsem, featsem, wsem, psem, rsem, g2sem, xfsem,
):
    nz, nx, ny = dims
    npat, nvis, ncode = visits_in.shape
    rank = core_ref.shape[0]
    half = ncode // 2
    ntile = pat_ref.shape[1]
    tile = ncode // ntile
    subj = lax.axis_index("subj")
    feat = lax.axis_index("feat")
    z = subj // (nx * ny)
    xh = (subj // ny) % nx
    y = subj % ny
    xlo, core = feat // 2, feat % 2

    def at(zz, xx, yy, ff):
        return {"subj": (zz * nx + xx) * ny + yy, "feat": ff}

    def zdev(d):
        return at((z + d + nz) % nz, xh, y, feat)

    def ydev(d):
        return at(z, xh, (y + d + ny) % ny, feat)

    xdev = at(z, 1 - xh, y, feat)

    sib = at(z, xh, y, xlo * 2 + 1 - core)
    over = at(z, xh, y, (1 - xlo) * 2 + core)

    def remote(src, dst, sems, i, dev):
        return pltpu.make_async_remote_copy(
            src_ref=src, dst_ref=dst, send_sem=sems.at[0, i], recv_sem=sems.at[1, i],
            device_id=dev, device_id_type=pl.DeviceIdType.MESH,
        )

    loads = [
        pltpu.make_async_copy(src, dst, lsem.at[i])
        for i, (src, dst) in enumerate((
            (codes_in, piece), (pat_in, pat_ref), (visits_in, vis),
            (cnt_in, cnt_ref), (core_in, core_ref), (pw_in, pw_ref),
        ))
    ]
    loads[0].start()
    barrier = pltpu.get_barrier_semaphore()
    partners = (
        [xdev, sib, over]
        + [ydev(d) for d in range(1, ny)] + [zdev(d) for d in range(1, nz)]
    )
    for dev in partners:
        pl.semaphore_signal(barrier, inc=1, device_id=dev, device_id_type=pl.DeviceIdType.MESH)
    for c in loads[1:]:
        c.start()
    pl.semaphore_wait(barrier, len(partners))

    loads[0].wait()
    g1 = []
    for d in range(1, ny):
        g1.append(remote(piece.at[:, pl.ds(0, half)], ga.at[y], g1sem, d, ydev(d)))
        g1[-1].start()
    for d in range(1, nz):
        g1.append(remote(piece.at[:, pl.ds(half, half)], gb.at[z], g1sem, ny + d, zdev(d)))
        g1[-1].start()
    ga[y] = piece[:, 0:half]
    gb[z] = piece[:, half:ncode]

    for c in loads[1:]:
        c.wait()
    mk[:, nvis:, :] = jnp.zeros((npat, VP - nvis, ncode), BF16)

    def mask_patient(k, carry):
        for t in range(ntile):
            cols = slice(t * tile, (t + 1) * tile)
            v = vis[k, :, cols]
            mk[k, 0:nvis, cols] = jnp.where(pat_ref[k, t] > 0, v, jnp.zeros_like(v))
        return carry

    lax.fori_loop(0, npat, mask_patient, 0)

    blk = 2 * nz * nx

    def natural(rp):
        yy, rest = rp // blk, rp % blk
        j, zi = rest // (2 * nz), rest % (2 * nz)
        return (zi // 2) * (2 * nx * ny) + j * (2 * ny) + yy * 2 + zi % 2

    rows = lax.broadcasted_iota(jnp.int32, (rank, rank), 0)
    cols = lax.broadcasted_iota(jnp.int32, (rank, rank), 1)
    to_nat[...] = jnp.where(rows == natural(cols), 1.0, 0.0).astype(BF16)
    to_b[...] = jnp.where(natural(rows) == cols, 1.0, 0.0).astype(BF16)

    axes = ((ca, z, nz, zdev), (cb, y, ny, ydev))
    pending = list(g1)
    live = {}
    planes = (xh, 1 - xh)

    def ring_copy(a, o, back, step, e):
        buf, me, n, dev = axes[a]
        block = buf.at[(me - back + n) % n, planes[o]]
        copy = remote(block, block, ringsem, (a * 2 + o) * 8 + e, dev(step))
        copy.start()
        pending.append(copy)
        return copy

    def spread(a, o):
        for e, k in enumerate(tree(axes[a][2], 1 - 2 * o)[0]):
            live[a, o, k] = ring_copy(a, o, 0, k, e)

    passed = set()

    def pass_on(a, o):
        first, later = tree(axes[a][2], 1 - 2 * o)
        for e, (k, step) in enumerate(later):
            if (a, o, k) not in passed:
                live[a, o, k].wait_recv()
                passed.add((a, o, k))
            live[a, o, k, step] = ring_copy(a, o, k, step, len(first) + e)

    xcopies = []

    def begin(a, count, got):
        buf, me, _, _ = axes[a]
        for s in range(count):
            rel[2 * s : 2 * s + 2, 0:half] = got[s].astype(F32)
        buf[me, xh] = rel[0 : 2 * count, 0:half].astype(BF16)
        block = buf.at[me, xh]
        xcopies.append(remote(block, block, xsem, a, xdev))
        xcopies[a].start()
        spread(a, 0)

    for c in g1[: ny - 1]:
        c.wait_recv()
    begin(0, ny, ga)
    for c in g1[ny - 1 :]:
        c.wait_recv()
    begin(1, nz, gb)
    pending += xcopies
    for a in (0, 1):
        pass_on(a, 0)
    for a in (0, 1):
        xcopies[a].wait_recv()
        spread(a, 1)
    for a in (0, 1):
        pass_on(a, 1)
    flat = npat * VP

    def all_here(a):
        for key in live:
            if key[0] == a and key not in passed:
                live[key].wait_recv()

    all_here(0)
    proj = lax.dot_general(
        mk[:, :, 0:half].reshape(flat, half), ca[...].reshape(rank, half), NT,
        preferred_element_type=F32,
    )
    all_here(1)
    cbn = mm(to_nat[...], cb[...].reshape(rank, half)).astype(BF16)
    proj = proj + lax.dot_general(
        mk[:, :, half:ncode].reshape(flat, half), cbn, NT, preferred_element_type=F32
    )
    own = flat // 4
    projf[...] = proj.reshape(2, 2, own, rank)

    fa = remote(projf.at[:, 1 - core], ra, featsem, 0, sib)
    fa.start()
    fa.wait()
    mine = (projf[:, core] + ra[...]).reshape(2 * own, rank)
    sb[...] = patient_codes(mine, nvis)
    fb = remote(sb, rb, featsem, 1, over)
    fb.start()
    mine = patient_values(sb[...], nvis)
    fb.wait()
    projected = mine + patient_values(rb[...], nvis)

    np_own = npat // 2
    rows_own = 2 * own

    def patient(p):
        return (p // (np_own // 2)) * (npat // 2) + core * (np_own // 2) + p % (np_own // 2)

    rowi = lax.broadcasted_iota(jnp.int32, (rows_own, rank), 0)
    limit = jnp.full((rows_own, rank), cnt_ref[patient(0)], jnp.int32)
    weights = jnp.broadcast_to(pw_ref[pl.ds(patient(0), 1), :], (rows_own, rank))
    for p in range(1, np_own):
        here = rowi >= p * VP
        limit = jnp.where(here, cnt_ref[patient(p)] + p * VP, limit)
        weights = jnp.where(here, pw_ref[pl.ds(patient(p), 1), :], weights)
    projected = jnp.where(rowi < limit, projected, 0.0)
    hi, lo = split2(projected * weights)
    core_w = core_ref[...]
    both = lax.dot_general(
        jnp.concatenate([hi, lo], axis=0), core_w, NT, preferred_element_type=F32
    )
    target = both[0:rows_own] + both[rows_own:]
    hi, lo = split2(target)
    lhs = jnp.concatenate([hi, lo, hi], axis=1)
    rhs = jnp.concatenate([hi, hi, lo], axis=1)
    blocks = [slice(b * own, (b + 1) * own) for b in range(2)]
    grams = [
        lax.dot_general(lhs[b], rhs[b], NT, preferred_element_type=F32) for b in blocks
    ]
    both = mm(jnp.concatenate([hi, lo], axis=0), core_w)
    base = both[0:rows_own] + both[rows_own:]
    square = jnp.sum(target * target, axis=1, keepdims=True)
    scale = jnp.zeros((rows_own, 1), F32)
    pi = lax.broadcasted_iota(jnp.int32, (rows_own, 1), 0) // VP
    for p in range(np_own):
        total = jnp.sum(square[p * VP : (p + 1) * VP], axis=0, keepdims=True)
        scale = jnp.where(pi == p, lax.rsqrt(total + 1e-06), scale)
    base = base * scale
    gi = lax.broadcasted_iota(jnp.int32, (own, own), 0)
    gj = lax.broadcasted_iota(jnp.int32, (own, own), 1)
    eye = jnp.where(gi == gj, 1.0, 0.0)
    grams = [
        jnp.where(gi // VP == gj // VP, g * (scale[b] * scale[b]), 0.0)
        for g, b in zip(grams, blocks)
    ]

    def grow(g, right):
        half_step = 1.5 * g - 0.5 * mm(left3(g), right)
        return 1.5 * half_step - 0.5 * mm(left3(half_step), right)

    polys = [1.5 * eye - 0.5 * g for g in grams]
    grams = [grow(g, right3(g)) for g in grams]

    def ns_step(i, carry):
        polys, grams = carry
        rights = [right3(g) for g in grams]
        polys = tuple(1.5 * p - 0.5 * mm(left3(p), r) for p, r in zip(polys, rights))
        return polys, tuple(grow(g, r) for g, r in zip(grams, rights))

    polys, grams = lax.fori_loop(0, NS_STEPS - 2, ns_step, (tuple(polys), tuple(grams)))
    rotated = jnp.concatenate(
        [
            mm(left3(1.5 * p - 0.5 * mm(left3(p), right3(g))), right3(base[b]))
            for p, g, b in zip(polys, grams, blocks)
        ],
        axis=0,
    )
    wbuf[core] = (rotated * weights).T.astype(BF16)
    beside = remote(wbuf.at[core], wbuf.at[core], wsem, 0, sib)
    beside.start()
    prod = rotated * projected
    for p in range(np_own):
        prow[core, p : p + 1, :] = jnp.sum(prod[p * VP : (p + 1) * VP], axis=0, keepdims=True)
    pcopies = [remote(prow.at[core], prow.at[core], psem, 0, sib)]
    for c in pcopies:
        c.start()
    beside.wait_recv()
    pending += [beside] + pcopies

    for f in range(4):
        wt[:, f * own : (f + 1) * own] = wbuf[f % 2, :, f // 2 * own : (f // 2 + 1) * own]
    wt_b = mm(to_b[...], wt[...]).astype(BF16)
    terms = (ta, tb)
    coded = ((qs_a, qr_a), (qs_b, qr_b))
    live = {}

    def send_sum(a, o, e, dest, step, extra):
        qs, qr = coded[a]
        v = terms[a][dest, planes[o]]
        for other in extra:
            live[a, o, other].wait_recv()
            v = v + values_of(qr[o, other])
        qs[o, e] = to_i16(codes_of(v))
        copy = remote(qs.at[o, e], qr.at[o, e], rsem, (a * 2 + o) * 8 + e, axes[a][3](-step))
        copy.start()
        live[a, o, e] = copy
        pending.append(copy)

    def leaves(a, o):
        _, me, n, _ = axes[a]
        first, later = tree(n, 1 - 2 * o)
        for e, (k, step) in enumerate(later):
            send_sum(a, o, len(first) + e, (me - k - step + n) % n, step, ())

    def inner(a, o, ready):
        _, me, n, _ = axes[a]
        first, later = tree(n, 1 - 2 * o)
        for e, k in enumerate(first):
            extra = [len(first) + ee for ee, (kk, _) in enumerate(later) if kk == k]
            if ready != bool(extra):
                send_sum(a, o, e, (me - k + n) % n, k, extra)

    def total(a, o):
        _, me, n, _ = axes[a]
        v = terms[a][me, planes[o]]
        for e in range(len(tree(n, 1)[0])):
            live[a, o, e].wait_recv()
            v = v + values_of(coded[a][1][o, e])
        return v

    ta[...] = mm(wt[...], mk[:, :, 0:half].reshape(flat, half)).reshape(ta.shape)
    leaves(0, 1)
    tb[...] = mm(wt_b, mk[:, :, half:ncode].reshape(flat, half)).reshape(tb.shape)
    leaves(1, 1)
    for a in (0, 1):
        inner(a, 1, True)
    for a in (0, 1):
        leaves(a, 0)
    for a in (0, 1):
        inner(a, 1, False)
    for a in (0, 1):
        inner(a, 0, True)
    for a in (0, 1):
        inner(a, 0, False)
    xsums = ((xs_a, xr_a), (xs_b, xr_b))
    xback = []
    for a in (0, 1):
        xsums[a][0][...] = to_i16(codes_of(total(a, 1)))
        xback.append(remote(xsums[a][0], xsums[a][1], xfsem, a, xdev))
        xback[a].start()
    owns = [total(a, 0) for a in (0, 1)]
    pending += xback
    last = []
    for a, (buf, got, dev, base) in enumerate(((s2a, r2a, ydev, 0), (s2b, r2b, zdev, ny))):
        xback[a].wait_recv()
        count, me = buf.shape[0], (y, z)[a]
        rel[0 : 2 * count, :] = codes_of(owns[a] + values_of(xsums[a][1][...]))
        for s in range(count):
            buf[s] = to_i16(rel[2 * s : 2 * s + 2, :])
        copies = []
        for d in range(1, count):
            copies.append(remote(buf.at[(me + d) % count], got.at[me], g2sem, base + d, dev(d)))
            copies[-1].start()
        last.append(copies)
        pending += copies
    for c in pcopies:
        c.wait_recv()
    pair = np_own // 2
    for f in range(4):
        out_pat[f * pair : (f + 1) * pair, :] = prow[f % 2, f // 2 * pair : (f // 2 + 1) * pair]
    for a, (buf, got) in enumerate(((s2a, r2a), (s2b, r2b))):
        count, me = buf.shape[0], (y, z)[a]
        for c in last[a]:
            c.wait_recv()
        v = values_of(buf[me])
        for d in range(1, count):
            v = v + values_of(got[(me + d) % count])
        out_codes[:, a * half : (a + 1) * half] = v
    for c in pending:
        c.wait_send()


def per_device(visits, tile_pattern, counts, codes_t, core, patient_weights, dims):
    nz, nx, ny = dims
    npat, nvis, ncode = visits.shape
    rank = core.shape[0]
    half = ncode // 2
    rows_a, rows_b = 2 * nx * ny, 2 * nz * nx
    flat = npat * VP
    own = flat // 4
    dma = pltpu.SemaphoreType.DMA
    vmem = pl.BlockSpec(memory_space=pltpu.VMEM)
    scratch = [
        pltpu.VMEM((npat, nvis, ncode), BF16),
        pltpu.SMEM(tile_pattern.shape, jnp.int32),
        pltpu.SMEM(counts.shape, jnp.int32),
        pltpu.VMEM(core.shape, BF16),
        pltpu.VMEM(patient_weights.shape, F32),
        pltpu.VMEM((npat, VP, ncode), BF16),
        pltpu.VMEM((2, ncode), BF16),
        pltpu.VMEM((ny, 2, half), BF16),
        pltpu.VMEM((nz, 2, half), BF16),
        pltpu.VMEM((max(rows_a, rows_b), half + 128), F32),
        pltpu.VMEM((nz, 2, rows_a // 2, half), BF16),
        pltpu.VMEM((ny, 2, rows_b // 2, half), BF16),
        pltpu.VMEM((2, 2, own, rank), F32),
        pltpu.VMEM((2, own, rank), F32),
        pltpu.VMEM((2 * own, rank), I16),
        pltpu.VMEM((2 * own, rank), I16),
        pltpu.VMEM((2, rank, 2 * own), BF16),
        pltpu.VMEM((2, npat // 2, rank), F32),
        pltpu.VMEM((rank, flat), BF16),
        pltpu.VMEM((rank, rank), BF16),
        pltpu.VMEM((rank, rank), BF16),
        pltpu.VMEM((nz, 2, rows_a // 2, half), F32),
        pltpu.VMEM((ny, 2, rows_b // 2, half), F32),
        pltpu.VMEM((2, 8, rows_a // 2, half + 128), I16),
        pltpu.VMEM((2, 8, rows_a // 2, half + 128), I16),
        pltpu.VMEM((2, 8, rows_b // 2, half + 128), I16),
        pltpu.VMEM((2, 8, rows_b // 2, half + 128), I16),
        pltpu.VMEM((ny, 2, half + 128), I16),
        pltpu.VMEM((ny, 2, half + 128), I16),
        pltpu.VMEM((nz, 2, half + 128), I16),
        pltpu.VMEM((nz, 2, half + 128), I16),
        pltpu.VMEM((rows_a // 2, half + 128), I16),
        pltpu.VMEM((rows_a // 2, half + 128), I16),
        pltpu.VMEM((rows_b // 2, half + 128), I16),
        pltpu.VMEM((rows_b // 2, half + 128), I16),
        dma((6,)),
        dma((2, 2)),
        dma((2, ny + nz)),
        dma((2, 32)),
        dma((2, 2)),
        dma((2, 1)),
        dma((2, 1)),
        dma((2, 32)),
        dma((2, ny + nz)),
        dma((2, 2)),
    ]
    return pl.pallas_call(
        functools.partial(kernel, dims),
        out_shape=(
            jax.ShapeDtypeStruct(codes_t.shape, F32),
            jax.ShapeDtypeStruct(patient_weights.shape, F32),
        ),
        in_specs=[pl.BlockSpec(memory_space=pltpu.HBM)] * 6,
        out_specs=(vmem, vmem),
        scratch_shapes=scratch,
        compiler_params=pltpu.CompilerParams(
            collective_id=0, has_side_effects=True, vmem_limit_bytes=60 * 1024 * 1024
        ),
        name="sweep",
    )(visits, tile_pattern, counts, codes_t, core, patient_weights)


def build(mesh, dims):
    return jax.shard_map(
        functools.partial(per_device, dims=dims),
        mesh=mesh,
        in_specs=(
            P("subj", None, "feat"),
            P("subj", "feat"),
            P("subj"),
            P("subj", "feat"),
            P(),
            P("subj", None),
        ),
        out_specs=(P("subj", "feat"), P("subj", None)),
        check_vma=False,
    )


def solution(mesh):
    return build(mesh, (NZ, NX, NY))
```

```python
import functools

import jax
import jax.numpy as jnp
from jax import lax
from jax.experimental import pallas as pl
from jax.experimental.pallas import tpu as pltpu
from jax.sharding import PartitionSpec as P

NS_STEPS = 8
NZ, NX, NY = 8, 2, 8
VP = 64
QMAX = 32000.0
F32 = jnp.float32
BF16 = jnp.bfloat16
I16 = jnp.int16
NT = (((1,), (1,)), ((), ()))


def split2(x):
    hi = x.astype(BF16)
    lo = (x - hi.astype(F32)).astype(BF16)
    return hi, lo


def left3(x):
    hi, lo = split2(x)
    return jnp.concatenate([hi, lo, hi], axis=1)


def right3(x):
    hi, lo = split2(x)
    return jnp.concatenate([hi, hi, lo], axis=0)


def mm(a, b):
    return jnp.dot(a, b, preferred_element_type=F32)


def tree(n, far):
    return {
        8: ((2, -2, 1, -1), ((2, 1), (-2, -1), (2 * far, 2 * far))),
        4: ((1, -1), ((far, far),)),
        2: ((1,), ()),
        1: ((), ()),
    }[n]


def encode(parts):
    top = jnp.abs(parts[0])
    for part in parts[1:]:
        top = jnp.maximum(top, jnp.abs(part))
    exponent = jnp.floor(jnp.log2(jnp.maximum(top, 1e-30))) + 1.0
    scale = jnp.exp2(-exponent) * QMAX
    return [jnp.round(part * scale) for part in parts] + [exponent]


def decode(parts):
    scale = jnp.exp2(parts[-1]) * (1.0 / QMAX)
    return [part * scale for part in parts[:-1]]


def to_i16(v):
    return v.astype(jnp.int32).astype(I16)


def from_i16(q):
    return q.astype(jnp.int32).astype(F32)


def tiles(v):
    return [v[..., c : c + 128] for c in range(0, v.shape[-1], 128)]


def codes_of(v):
    return jnp.concatenate(encode(tiles(v)), axis=-1)


def values_of(q):
    return jnp.concatenate(decode(tiles(from_i16(q))), axis=-1)


def patient_codes(v, nvis):
    out = []
    for p in range(0, v.shape[0], VP):
        out += encode([v[p + r : p + r + 8] for r in range(0, nvis, 8)])
    return to_i16(jnp.concatenate(out, axis=0))


def patient_values(q, nvis):
    v = from_i16(q)
    out = []
    for p in range(0, v.shape[0], VP):
        out += decode([v[p + r : p + r + 8] for r in range(0, nvis + 8, 8)])
        out.append(jnp.zeros((8, v.shape[1]), F32))
    return jnp.concatenate(out, axis=0)


def kernel(
    dims,
    visits_in, pat_in, cnt_in, codes_in, core_in, pw_in,
    out_codes, out_pat,
    vis, pat_ref, cnt_ref, core_ref, pw_ref, mk, piece, ga, gb, piece2, ga2, gb2, rel, ca, cb, projf, ra, rb, sb, wbuf, prow, wt, to_nat, to_b, ta, tb,
    qs_a, qr_a, qs_b, qr_b, s2a, r2a, s2b, r2b, xs_a, xr_a, xs_b, xr_b,
    lsem, xsem, g1sem, ringsem, featsem, wsem, psem, rsem, g2sem, xfsem,
):
    nz, nx, ny = dims
    npat, nvis, ncode = visits_in.shape
    rank = core_ref.shape[0]
    half = ncode // 2
    ntile = pat_ref.shape[1]
    tile = ncode // ntile
    subj = lax.axis_index("subj")
    feat = lax.axis_index("feat")
    z = subj // (nx * ny)
    xh = (subj // ny) % nx
    y = subj % ny
    xlo, core = feat // 2, feat % 2

    def at(zz, xx, yy, ff):
        return {"subj": (zz * nx + xx) * ny + yy, "feat": ff}

    def zdev(d):
        return at((z + d + nz) % nz, xh, y, feat)

    def ydev(d):
        return at(z, xh, (y + d + ny) % ny, feat)

    xdev = at(z, 1 - xh, y, feat)

    sib = at(z, xh, y, xlo * 2 + 1 - core)
    over = at(z, xh, y, (1 - xlo) * 2 + core)

    def remote(src, dst, sems, i, dev):
        return pltpu.make_async_remote_copy(
            src_ref=src, dst_ref=dst, send_sem=sems.at[0, i], recv_sem=sems.at[1, i],
            device_id=dev, device_id_type=pl.DeviceIdType.MESH,
        )

    loads = [
        pltpu.make_async_copy(src, dst, lsem.at[i])
        for i, (src, dst) in enumerate((
            (codes_in, piece), (pat_in, pat_ref), (visits_in, vis),
            (cnt_in, cnt_ref), (core_in, core_ref), (pw_in, pw_ref),
        ))
    ]
    loads[0].start()
    barrier = pltpu.get_barrier_semaphore()
    partners = (
        [xdev, sib, over]
        + [ydev(d) for d in range(1, ny)] + [zdev(d) for d in range(1, nz)]
    )
    for dev in partners:
        pl.semaphore_signal(barrier, inc=1, device_id=dev, device_id_type=pl.DeviceIdType.MESH)
    for c in loads[1:]:
        c.start()
    pl.semaphore_wait(barrier, len(partners))

    loads[0].wait()
    xcopy = remote(piece, piece2, xsem, 0, xdev)
    xcopy.start()

    def scatter(src, got_a, got_b, base):
        copies = []
        for d in range(1, ny):
            copies.append(remote(src.at[:, pl.ds(0, half)], got_a.at[y], g1sem, base + d, ydev(d)))
            copies[-1].start()
        for d in range(1, nz):
            copies.append(
                remote(src.at[:, pl.ds(half, half)], got_b.at[z], g1sem, base + ny + d, zdev(d))
            )
            copies[-1].start()
        got_a[y] = src[:, 0:half]
        got_b[z] = src[:, half:ncode]
        return copies

    g1 = scatter(piece, ga, gb, 0)
    xcopy.wait_recv()
    g2 = scatter(piece2, ga2, gb2, ny + nz)

    for c in loads[1:]:
        c.wait()
    mk[:, nvis:, :] = jnp.zeros((npat, VP - nvis, ncode), BF16)

    def mask_patient(k, carry):
        for t in range(ntile):
            cols = slice(t * tile, (t + 1) * tile)
            v = vis[k, :, cols]
            mk[k, 0:nvis, cols] = jnp.where(pat_ref[k, t] > 0, v, jnp.zeros_like(v))
        return carry

    lax.fori_loop(0, npat, mask_patient, 0)

    blk = 2 * nz * nx

    def natural(rp):
        yy, rest = rp // blk, rp % blk
        j, zi = rest // (2 * nz), rest % (2 * nz)
        return (zi // 2) * (2 * nx * ny) + j * (2 * ny) + yy * 2 + zi % 2

    rows = lax.broadcasted_iota(jnp.int32, (rank, rank), 0)
    cols = lax.broadcasted_iota(jnp.int32, (rank, rank), 1)
    to_nat[...] = jnp.where(rows == natural(cols), 1.0, 0.0).astype(BF16)
    to_b[...] = jnp.where(natural(rows) == cols, 1.0, 0.0).astype(BF16)

    axes = ((ca, z, nz, zdev), (cb, y, ny, ydev))
    pending = g1 + g2 + [xcopy]
    live = {}
    planes = (xh, 1 - xh)

    def ring_copy(a, o, back, step, e):
        buf, me, n, dev = axes[a]
        block = buf.at[(me - back + n) % n, planes[o]]
        copy = remote(block, block, ringsem, (a * 2 + o) * 8 + e, dev(step))
        copy.start()
        pending.append(copy)
        return copy

    def spread(a, o):
        for e, k in enumerate(tree(axes[a][2], 1 - 2 * o)[0]):
            live[a, o, k] = ring_copy(a, o, 0, k, e)

    passed = set()

    def pass_on(a, o):
        first, later = tree(axes[a][2], 1 - 2 * o)
        for e, (k, step) in enumerate(later):
            if (a, o, k) not in passed:
                live[a, o, k].wait_recv()
                passed.add((a, o, k))
            live[a, o, k, step] = ring_copy(a, o, k, step, len(first) + e)

    def begin(a, o, count, got):
        buf, me, _, _ = axes[a]
        for s in range(count):
            rel[2 * s : 2 * s + 2, 0:half] = got[s].astype(F32)
        buf[me, planes[o]] = rel[0 : 2 * count, 0:half].astype(BF16)
        spread(a, o)

    for c in g1[: ny - 1]:
        c.wait_recv()
    begin(0, 0, ny, ga)
    for c in g1[ny - 1 :]:
        c.wait_recv()
    begin(1, 0, nz, gb)
    for c in g2[: ny - 1]:
        c.wait_recv()
    begin(0, 1, ny, ga2)
    for c in g2[ny - 1 :]:
        c.wait_recv()
    begin(1, 1, nz, gb2)
    for a in (0, 1):
        pass_on(a, 0)
    for a in (0, 1):
        pass_on(a, 1)
    flat = npat * VP

    def all_here(a):
        for key in live:
            if key[0] == a and key not in passed:
                live[key].wait_recv()

    all_here(0)
    proj = lax.dot_general(
        mk[:, :, 0:half].reshape(flat, half), ca[...].reshape(rank, half), NT,
        preferred_element_type=F32,
    )
    all_here(1)
    cbn = mm(to_nat[...], cb[...].reshape(rank, half)).astype(BF16)
    proj = proj + lax.dot_general(
        mk[:, :, half:ncode].reshape(flat, half), cbn, NT, preferred_element_type=F32
    )
    own = flat // 4
    projf[...] = proj.reshape(2, 2, own, rank)

    fa = [remote(projf.at[b, 1 - core], ra.at[b], featsem, b, sib) for b in range(2)]
    fb = [remote(sb.at[b], rb.at[b], featsem, 2 + b, over) for b in range(2)]
    for b in range(2):
        fa[b].start()
    for b in range(2):
        fa[b].wait_recv()
        sb[b] = patient_codes(projf[b, core] + ra[b], nvis)
        fb[b].start()
    pending += fa + fb

    np_own = npat // 2
    pair = np_own // 2
    core_w = core_ref[...]
    rowi = lax.broadcasted_iota(jnp.int32, (own, rank), 0)
    pi = lax.broadcasted_iota(jnp.int32, (own, 1), 0) // VP
    gi = lax.broadcasted_iota(jnp.int32, (own, own), 0)
    gj = lax.broadcasted_iota(jnp.int32, (own, own), 1)
    eye = jnp.where(gi == gj, 1.0, 0.0)

    def block_setup(b):
        first = b * (npat // 2) + core * pair
        limit = jnp.full((own, rank), cnt_ref[first], jnp.int32)
        weights = jnp.broadcast_to(pw_ref[pl.ds(first, 1), :], (own, rank))
        for p in range(1, pair):
            here = rowi >= p * VP
            limit = jnp.where(here, cnt_ref[first + p] + p * VP, limit)
            weights = jnp.where(here, pw_ref[pl.ds(first + p, 1), :], weights)
        mine = patient_values(sb[b], nvis)
        fb[b].wait_recv()
        projected = jnp.where(rowi < limit, mine + patient_values(rb[b], nvis), 0.0)
        both = lax.dot_general(
            jnp.concatenate(split2(projected * weights), axis=0), core_w, NT,
            preferred_element_type=F32,
        )
        target = both[0:own] + both[own:]
        hi, lo = split2(target)
        gram = lax.dot_general(
            jnp.concatenate([hi, lo, hi], axis=1), jnp.concatenate([hi, hi, lo], axis=1), NT,
            preferred_element_type=F32,
        )
        both = mm(jnp.concatenate([hi, lo], axis=0), core_w)
        square = jnp.sum(target * target, axis=1, keepdims=True)
        scale = jnp.zeros((own, 1), F32)
        for p in range(pair):
            total = jnp.sum(square[p * VP : (p + 1) * VP], axis=0, keepdims=True)
            scale = jnp.where(pi == p, lax.rsqrt(total + 1e-06), scale)
        base = (both[0:own] + both[own:]) * scale
        gram = jnp.where(gi // VP == gj // VP, gram * (scale * scale), 0.0)
        return projected, weights, base, gram

    setups = [block_setup(b) for b in range(2)]
    grams = [s[3] for s in setups]

    def grow(g, right):
        half_step = 1.5 * g - 0.5 * mm(left3(g), right)
        return 1.5 * half_step - 0.5 * mm(left3(half_step), right)

    polys = [1.5 * eye - 0.5 * g for g in grams]
    grams = [grow(g, right3(g)) for g in grams]

    def product(rows, right):
        both = mm(rows, right)
        both = both[:, 0:own] + both[:, own:]
        return [
            both[i : i + own] + both[i + own : i + 2 * own] for i in range(0, rows.shape[0], 2 * own)
        ]

    def ns_block(p, g):
        parts = split2(g)
        right = jnp.concatenate(parts, axis=1)
        half_step = 1.5 * g - 0.5 * product(jnp.concatenate(parts, axis=0), right)[0]
        rows = jnp.concatenate(split2(half_step) + split2(p), axis=0)
        grown, moved = product(rows, right)
        return 1.5 * p - 0.5 * moved, 1.5 * half_step - 0.5 * grown

    def ns_step(i, carry):
        done = [ns_block(p, g) for p, g in zip(*carry)]
        return tuple(p for p, _ in done), tuple(g for _, g in done)

    for i in range(NS_STEPS - 2):
        polys, grams = ns_step(i, (polys, grams))
    beside = []
    rotateds = []
    for b in range(2):
        _, weights, base, _ = setups[b]
        poly = 1.5 * polys[b] - 0.5 * mm(left3(polys[b]), right3(grams[b]))
        rotated = mm(left3(poly), right3(base))
        rotateds.append(rotated)
        wbuf[core, b] = (rotated * weights).T.astype(BF16)
        beside.append(remote(wbuf.at[core, b], wbuf.at[core, b], wsem, b, sib))
        beside[b].start()
    for b in range(2):
        prod = rotateds[b] * setups[b][0]
        for p in range(pair):
            row = jnp.sum(prod[p * VP : (p + 1) * VP], axis=0, keepdims=True)
            prow[core, b * pair + p : b * pair + p + 1, :] = row
    pcopies = [remote(prow.at[core], prow.at[core], psem, 0, sib)]
    for c in pcopies:
        c.start()
    for c in beside:
        c.wait_recv()
    pending += beside + pcopies

    for f in range(4):
        wt[:, f * own : (f + 1) * own] = wbuf[f % 2, f // 2]
    wt_b = mm(to_b[...], wt[...]).astype(BF16)
    terms = (ta, tb)
    coded = ((qs_a, qr_a), (qs_b, qr_b))
    live = {}

    def send_sum(a, o, e, dest, step, extra):
        qs, qr = coded[a]
        v = terms[a][dest, planes[o]]
        for other in extra:
            live[a, o, other].wait_recv()
            v = v + values_of(qr[o, other])
        qs[o, e] = to_i16(codes_of(v))
        copy = remote(qs.at[o, e], qr.at[o, e], rsem, (a * 2 + o) * 8 + e, axes[a][3](-step))
        copy.start()
        live[a, o, e] = copy
        pending.append(copy)

    def leaves(a, o):
        _, me, n, _ = axes[a]
        first, later = tree(n, 1 - 2 * o)
        for e, (k, step) in enumerate(later):
            send_sum(a, o, len(first) + e, (me - k - step + n) % n, step, ())

    def inner(a, o, ready):
        _, me, n, _ = axes[a]
        first, later = tree(n, 1 - 2 * o)
        for e, k in enumerate(first):
            extra = [len(first) + ee for ee, (kk, _) in enumerate(later) if kk == k]
            if ready != bool(extra):
                send_sum(a, o, e, (me - k + n) % n, k, extra)

    def total(a, o):
        _, me, n, _ = axes[a]
        v = terms[a][me, planes[o]]
        for e in range(len(tree(n, 1)[0])):
            live[a, o, e].wait_recv()
            v = v + values_of(coded[a][1][o, e])
        return v

    ta[...] = mm(wt[...], mk[:, :, 0:half].reshape(flat, half)).reshape(ta.shape)
    leaves(0, 1)
    tb[...] = mm(wt_b, mk[:, :, half:ncode].reshape(flat, half)).reshape(tb.shape)
    leaves(1, 1)
    for a in (0, 1):
        inner(a, 1, True)
    for a in (0, 1):
        leaves(a, 0)
    for a in (0, 1):
        inner(a, 1, False)
    for a in (0, 1):
        inner(a, 0, True)
    for a in (0, 1):
        inner(a, 0, False)
    xsums = ((xs_a, xr_a), (xs_b, xr_b))
    xback = []
    for a in (0, 1):
        xsums[a][0][...] = to_i16(codes_of(total(a, 1)))
        xback.append(remote(xsums[a][0], xsums[a][1], xfsem, a, xdev))
        xback[a].start()
    owns = [total(a, 0) for a in (0, 1)]
    pending += xback
    last = []
    for a, (buf, got, dev, base) in enumerate(((s2a, r2a, ydev, 0), (s2b, r2b, zdev, ny))):
        xback[a].wait_recv()
        count, me = buf.shape[0], (y, z)[a]
        rel[0 : 2 * count, :] = codes_of(owns[a] + values_of(xsums[a][1][...]))
        for s in range(count):
            buf[s] = to_i16(rel[2 * s : 2 * s + 2, :])
        copies = []
        for d in range(1, count):
            copies.append(remote(buf.at[(me + d) % count], got.at[me], g2sem, base + d, dev(d)))
            copies[-1].start()
        last.append(copies)
        pending += copies
    for c in pcopies:
        c.wait_recv()
    for f in range(4):
        out_pat[f * pair : (f + 1) * pair, :] = prow[f % 2, f // 2 * pair : (f // 2 + 1) * pair]
    for a, (buf, got) in enumerate(((s2a, r2a), (s2b, r2b))):
        count, me = buf.shape[0], (y, z)[a]
        for c in last[a]:
            c.wait_recv()
        v = values_of(buf[me])
        for d in range(1, count):
            v = v + values_of(got[(me + d) % count])
        out_codes[:, a * half : (a + 1) * half] = v
    for c in pending:
        c.wait_send()


def per_device(visits, tile_pattern, counts, codes_t, core, patient_weights, dims):
    nz, nx, ny = dims
    npat, nvis, ncode = visits.shape
    rank = core.shape[0]
    half = ncode // 2
    rows_a, rows_b = 2 * nx * ny, 2 * nz * nx
    flat = npat * VP
    own = flat // 4
    dma = pltpu.SemaphoreType.DMA
    vmem = pl.BlockSpec(memory_space=pltpu.VMEM)
    scratch = [
        pltpu.VMEM((npat, nvis, ncode), BF16),
        pltpu.SMEM(tile_pattern.shape, jnp.int32),
        pltpu.SMEM(counts.shape, jnp.int32),
        pltpu.VMEM(core.shape, BF16),
        pltpu.VMEM(patient_weights.shape, F32),
        pltpu.VMEM((npat, VP, ncode), BF16),
        pltpu.VMEM((2, ncode), BF16),
        pltpu.VMEM((ny, 2, half), BF16),
        pltpu.VMEM((nz, 2, half), BF16),
        pltpu.VMEM((2, ncode), BF16),
        pltpu.VMEM((ny, 2, half), BF16),
        pltpu.VMEM((nz, 2, half), BF16),
        pltpu.VMEM((max(rows_a, rows_b), half + 128), F32),
        pltpu.VMEM((nz, 2, rows_a // 2, half), BF16),
        pltpu.VMEM((ny, 2, rows_b // 2, half), BF16),
        pltpu.VMEM((2, 2, own, rank), F32),
        pltpu.VMEM((2, own, rank), F32),
        pltpu.VMEM((2, own, rank), I16),
        pltpu.VMEM((2, own, rank), I16),
        pltpu.VMEM((2, 2, rank, own), BF16),
        pltpu.VMEM((2, npat // 2, rank), F32),
        pltpu.VMEM((rank, flat), BF16),
        pltpu.VMEM((rank, rank), BF16),
        pltpu.VMEM((rank, rank), BF16),
        pltpu.VMEM((nz, 2, rows_a // 2, half), F32),
        pltpu.VMEM((ny, 2, rows_b // 2, half), F32),
        pltpu.VMEM((2, 8, rows_a // 2, half + 128), I16),
        pltpu.VMEM((2, 8, rows_a // 2, half + 128), I16),
        pltpu.VMEM((2, 8, rows_b // 2, half + 128), I16),
        pltpu.VMEM((2, 8, rows_b // 2, half + 128), I16),
        pltpu.VMEM((ny, 2, half + 128), I16),
        pltpu.VMEM((ny, 2, half + 128), I16),
        pltpu.VMEM((nz, 2, half + 128), I16),
        pltpu.VMEM((nz, 2, half + 128), I16),
        pltpu.VMEM((rows_a // 2, half + 128), I16),
        pltpu.VMEM((rows_a // 2, half + 128), I16),
        pltpu.VMEM((rows_b // 2, half + 128), I16),
        pltpu.VMEM((rows_b // 2, half + 128), I16),
        dma((6,)),
        dma((2, 1)),
        dma((2, 2 * (ny + nz))),
        dma((2, 32)),
        dma((2, 4)),
        dma((2, 2)),
        dma((2, 1)),
        dma((2, 32)),
        dma((2, ny + nz)),
        dma((2, 2)),
    ]
    return pl.pallas_call(
        functools.partial(kernel, dims),
        out_shape=(
            jax.ShapeDtypeStruct(codes_t.shape, F32),
            jax.ShapeDtypeStruct(patient_weights.shape, F32),
        ),
        in_specs=[pl.BlockSpec(memory_space=pltpu.HBM)] * 6,
        out_specs=(vmem, vmem),
        scratch_shapes=scratch,
        compiler_params=pltpu.CompilerParams(
            collective_id=0, has_side_effects=True, vmem_limit_bytes=60 * 1024 * 1024
        ),
        name="sweep",
    )(visits, tile_pattern, counts, codes_t, core, patient_weights)


def build(mesh, dims):
    return jax.shard_map(
        functools.partial(per_device, dims=dims),
        mesh=mesh,
        in_specs=(
            P("subj", None, "feat"),
            P("subj", "feat"),
            P("subj"),
            P("subj", "feat"),
            P(),
            P("subj", None),
        ),
        out_specs=(P("subj", "feat"), P("subj", None)),
        check_vma=False,
    )


def solution(mesh):
    return build(mesh, (NZ, NX, NY))
```

```python
import functools

import jax
import jax.numpy as jnp
from jax import lax
from jax.experimental import pallas as pl
from jax.experimental.pallas import tpu as pltpu
from jax.sharding import PartitionSpec as P

NS_STEPS = 8
NZ, NX, NY = 8, 2, 8
VP = 64
QMAX = 32000.0
F32 = jnp.float32
BF16 = jnp.bfloat16
I16 = jnp.int16
NT = (((1,), (1,)), ((), ()))


def split2(x):
    hi = x.astype(BF16)
    lo = (x - hi.astype(F32)).astype(BF16)
    return hi, lo


def left3(x):
    hi, lo = split2(x)
    return jnp.concatenate([hi, lo, hi], axis=1)


def right3(x):
    hi, lo = split2(x)
    return jnp.concatenate([hi, hi, lo], axis=0)


def mm(a, b):
    return jnp.dot(a, b, preferred_element_type=F32)


def tree(n, far):
    return {
        8: ((2, -2, 1, -1), ((2, 1), (-2, -1), (2 * far, 2 * far))),
        4: ((1, -1), ((far, far),)),
        2: ((1,), ()),
        1: ((), ()),
    }[n]


def encode(parts):
    top = jnp.abs(parts[0])
    for part in parts[1:]:
        top = jnp.maximum(top, jnp.abs(part))
    exponent = jnp.floor(jnp.log2(jnp.maximum(top, 1e-30))) + 1.0
    scale = jnp.exp2(-exponent) * QMAX
    return [jnp.round(part * scale) for part in parts] + [exponent]


def decode(parts):
    scale = jnp.exp2(parts[-1]) * (1.0 / QMAX)
    return [part * scale for part in parts[:-1]]


def to_i16(v):
    return v.astype(jnp.int32).astype(I16)


def from_i16(q):
    return q.astype(jnp.int32).astype(F32)


def tiles(v):
    return [v[..., c : c + 128] for c in range(0, v.shape[-1], 128)]


def codes_of(v):
    return jnp.concatenate(encode(tiles(v)), axis=-1)


def values_of(q):
    return jnp.concatenate(decode(tiles(from_i16(q))), axis=-1)


def patient_codes(v, nvis):
    out = []
    for p in range(0, v.shape[0], VP):
        out += encode([v[p + r : p + r + 8] for r in range(0, nvis, 8)])
    return to_i16(jnp.concatenate(out, axis=0))


def patient_values(q, nvis):
    v = from_i16(q)
    out = []
    for p in range(0, v.shape[0], VP):
        out += decode([v[p + r : p + r + 8] for r in range(0, nvis + 8, 8)])
        out.append(jnp.zeros((8, v.shape[1]), F32))
    return jnp.concatenate(out, axis=0)


def kernel(
    dims,
    visits_in, pat_in, cnt_in, codes_in, core_in, pw_in,
    out_codes, out_pat,
    vis, pat_ref, cnt_ref, core_ref, pw_ref, mk, piece, ga, gb, piece2, ga2, gb2, rel, ca, cb, projf, ra, rb, sb, wbuf, prow, wt, wtb, to_nat, to_b, ta, tb,
    qs_a, qr_a, qs_b, qr_b, s2a, r2a, s2b, r2b, xs_a, xr_a, xs_b, xr_b,
    lsem, xsem, g1sem, ringsem, featsem, wsem, psem, rsem, g2sem, xfsem,
):
    nz, nx, ny = dims
    npat, nvis, ncode = visits_in.shape
    rank = core_ref.shape[0]
    half = ncode // 2
    ntile = pat_ref.shape[1]
    tile = ncode // ntile
    subj = lax.axis_index("subj")
    feat = lax.axis_index("feat")
    z = subj // (nx * ny)
    xh = (subj // ny) % nx
    y = subj % ny
    xlo, core = feat // 2, feat % 2

    def at(zz, xx, yy, ff):
        return {"subj": (zz * nx + xx) * ny + yy, "feat": ff}

    def zdev(d):
        return at((z + d + nz) % nz, xh, y, feat)

    def ydev(d):
        return at(z, xh, (y + d + ny) % ny, feat)

    xdev = at(z, 1 - xh, y, feat)

    sib = at(z, xh, y, xlo * 2 + 1 - core)
    over = at(z, xh, y, (1 - xlo) * 2 + core)

    def remote(src, dst, sems, i, dev):
        return pltpu.make_async_remote_copy(
            src_ref=src, dst_ref=dst, send_sem=sems.at[0, i], recv_sem=sems.at[1, i],
            device_id=dev, device_id_type=pl.DeviceIdType.MESH,
        )

    loads = [
        pltpu.make_async_copy(src, dst, lsem.at[i])
        for i, (src, dst) in enumerate((
            (codes_in, piece), (pat_in, pat_ref), (visits_in, vis),
            (cnt_in, cnt_ref), (core_in, core_ref), (pw_in, pw_ref),
        ))
    ]
    loads[0].start()
    barrier = pltpu.get_barrier_semaphore()
    partners = (
        [xdev, sib, over]
        + [ydev(d) for d in range(1, ny)] + [zdev(d) for d in range(1, nz)]
    )
    for dev in partners:
        pl.semaphore_signal(barrier, inc=1, device_id=dev, device_id_type=pl.DeviceIdType.MESH)
    for c in loads[1:]:
        c.start()
    pl.semaphore_wait(barrier, len(partners))

    loads[0].wait()
    xcopy = remote(piece, piece2, xsem, 0, xdev)
    xcopy.start()

    def scatter(src, got_a, got_b, base):
        copies = []
        for d in range(1, ny):
            copies.append(remote(src.at[:, pl.ds(0, half)], got_a.at[y], g1sem, base + d, ydev(d)))
            copies[-1].start()
        for d in range(1, nz):
            copies.append(
                remote(src.at[:, pl.ds(half, half)], got_b.at[z], g1sem, base + ny + d, zdev(d))
            )
            copies[-1].start()
        got_a[y] = src[:, 0:half]
        got_b[z] = src[:, half:ncode]
        return copies

    g1 = scatter(piece, ga, gb, 0)
    xcopy.wait_recv()
    g2 = scatter(piece2, ga2, gb2, ny + nz)

    for c in loads[1:]:
        c.wait()
    mk[:, nvis:, :] = jnp.zeros((npat, VP - nvis, ncode), BF16)

    def mask_patient(k, carry):
        for t in range(ntile):
            cols = slice(t * tile, (t + 1) * tile)
            v = vis[k, :, cols]
            mk[k, 0:nvis, cols] = jnp.where(pat_ref[k, t] > 0, v, jnp.zeros_like(v))
        return carry

    lax.fori_loop(0, npat, mask_patient, 0)

    blk = 2 * nz * nx

    def natural(rp):
        yy, rest = rp // blk, rp % blk
        j, zi = rest // (2 * nz), rest % (2 * nz)
        return (zi // 2) * (2 * nx * ny) + j * (2 * ny) + yy * 2 + zi % 2

    rows = lax.broadcasted_iota(jnp.int32, (rank, rank), 0)
    cols = lax.broadcasted_iota(jnp.int32, (rank, rank), 1)
    to_nat[...] = jnp.where(rows == natural(cols), 1.0, 0.0).astype(BF16)
    to_b[...] = jnp.where(natural(rows) == cols, 1.0, 0.0).astype(BF16)

    axes = ((ca, z, nz, zdev), (cb, y, ny, ydev))
    pending = g1 + g2 + [xcopy]
    live = {}
    planes = (xh, 1 - xh)

    def ring_copy(a, o, back, step, e):
        buf, me, n, dev = axes[a]
        block = buf.at[(me - back + n) % n, planes[o]]
        copy = remote(block, block, ringsem, (a * 2 + o) * 8 + e, dev(step))
        copy.start()
        pending.append(copy)
        return copy

    def spread(a, o):
        for e, k in enumerate(tree(axes[a][2], 1 - 2 * o)[0]):
            live[a, o, k] = ring_copy(a, o, 0, k, e)

    passed = set()

    def pass_on(a, o):
        first, later = tree(axes[a][2], 1 - 2 * o)
        for e, (k, step) in enumerate(later):
            if (a, o, k) not in passed:
                live[a, o, k].wait_recv()
                passed.add((a, o, k))
            live[a, o, k, step] = ring_copy(a, o, k, step, len(first) + e)

    def begin(a, o, count, got):
        buf, me, _, _ = axes[a]
        for s in range(count):
            rel[2 * s : 2 * s + 2, 0:half] = got[s].astype(F32)
        buf[me, planes[o]] = rel[0 : 2 * count, 0:half].astype(BF16)
        spread(a, o)

    for c in g1[: ny - 1]:
        c.wait_recv()
    begin(0, 0, ny, ga)
    for c in g1[ny - 1 :]:
        c.wait_recv()
    begin(1, 0, nz, gb)
    for c in g2[: ny - 1]:
        c.wait_recv()
    begin(0, 1, ny, ga2)
    for c in g2[ny - 1 :]:
        c.wait_recv()
    begin(1, 1, nz, gb2)
    for a in (0, 1):
        pass_on(a, 0)
    for a in (0, 1):
        pass_on(a, 1)
    flat = npat * VP

    def all_here(a):
        for key in live:
            if key[0] == a and key not in passed:
                live[key].wait_recv()

    all_here(0)
    proj = lax.dot_general(
        mk[:, :, 0:half].reshape(flat, half), ca[...].reshape(rank, half), NT,
        preferred_element_type=F32,
    )
    all_here(1)
    cbn = mm(to_nat[...], cb[...].reshape(rank, half)).astype(BF16)
    own = flat // 4
    fa = [remote(projf.at[b, 1 - core], ra.at[b], featsem, b, sib) for b in range(2)]
    fb = [remote(sb.at[b], rb.at[b], featsem, 2 + b, over) for b in range(2)]
    for b in range(2):
        rows = slice(b * npat // 2, (b + 1) * npat // 2)
        block = proj[b * 2 * own : (b + 1) * 2 * own] + lax.dot_general(
            mk[rows, :, half:ncode].reshape(2 * own, half), cbn, NT, preferred_element_type=F32
        )
        projf[b] = block.reshape(2, own, rank)
        fa[b].start()
    for b in range(2):
        fa[b].wait_recv()
        sb[b] = patient_codes(projf[b, core] + ra[b], nvis)
        fb[b].start()
    pending += fa + fb

    np_own = npat // 2
    pair = np_own // 2
    core_w = core_ref[...]
    rowi = lax.broadcasted_iota(jnp.int32, (own, rank), 0)
    pi = lax.broadcasted_iota(jnp.int32, (own, 1), 0) // VP
    gi = lax.broadcasted_iota(jnp.int32, (own, own), 0)
    gj = lax.broadcasted_iota(jnp.int32, (own, own), 1)
    eye = jnp.where(gi == gj, 1.0, 0.0)

    def block_setup(b):
        first = b * (npat // 2) + core * pair
        limit = jnp.full((own, rank), cnt_ref[first], jnp.int32)
        weights = jnp.broadcast_to(pw_ref[pl.ds(first, 1), :], (own, rank))
        for p in range(1, pair):
            here = rowi >= p * VP
            limit = jnp.where(here, cnt_ref[first + p] + p * VP, limit)
            weights = jnp.where(here, pw_ref[pl.ds(first + p, 1), :], weights)
        mine = patient_values(sb[b], nvis)
        fb[b].wait_recv()
        projected = jnp.where(rowi < limit, mine + patient_values(rb[b], nvis), 0.0)
        both = lax.dot_general(
            jnp.concatenate(split2(projected * weights), axis=0), core_w, NT,
            preferred_element_type=F32,
        )
        target = both[0:own] + both[own:]
        hi, lo = split2(target)
        gram = lax.dot_general(
            jnp.concatenate([hi, lo, hi], axis=1), jnp.concatenate([hi, hi, lo], axis=1), NT,
            preferred_element_type=F32,
        )
        both = mm(jnp.concatenate([hi, lo], axis=0), core_w)
        square = jnp.sum(target * target, axis=1, keepdims=True)
        scale = jnp.zeros((own, 1), F32)
        for p in range(pair):
            total = jnp.sum(square[p * VP : (p + 1) * VP], axis=0, keepdims=True)
            scale = jnp.where(pi == p, lax.rsqrt(total + 1e-06), scale)
        base = (both[0:own] + both[own:]) * scale
        gram = jnp.where(gi // VP == gj // VP, gram * (scale * scale), 0.0)
        return projected, weights, base, gram

    setups = [block_setup(b) for b in range(2)]
    grams = [s[3] for s in setups]

    def grow(g, right):
        half_step = 1.5 * g - 0.5 * mm(left3(g), right)
        return 1.5 * half_step - 0.5 * mm(left3(half_step), right)

    polys = [1.5 * eye - 0.5 * g for g in grams]
    grams = [grow(g, right3(g)) for g in grams]

    def product(rows, right):
        both = mm(rows, right)
        both = both[:, 0:own] + both[:, own:]
        return [
            both[i : i + own] + both[i + own : i + 2 * own] for i in range(0, rows.shape[0], 2 * own)
        ]

    def ns_block(p, g):
        parts = split2(g)
        right = jnp.concatenate(parts, axis=1)
        half_step = 1.5 * g - 0.5 * product(jnp.concatenate(parts, axis=0), right)[0]
        rows = jnp.concatenate(split2(half_step) + split2(p), axis=0)
        grown, moved = product(rows, right)
        return 1.5 * p - 0.5 * moved, 1.5 * half_step - 0.5 * grown

    def ns_step(i, carry):
        done = [ns_block(p, g) for p, g in zip(*carry)]
        return tuple(p for p, _ in done), tuple(g for _, g in done)

    for i in range(NS_STEPS - 2):
        polys, grams = ns_step(i, (polys, grams))
    beside = []
    rotateds = []
    for b in range(2):
        _, weights, base, _ = setups[b]
        poly = 1.5 * polys[b] - 0.5 * mm(left3(polys[b]), right3(grams[b]))
        rotated = mm(left3(poly), right3(base))
        rotateds.append(rotated)
        wbuf[core, b] = (rotated * weights).T.astype(BF16)
        beside.append(remote(wbuf.at[core, b], wbuf.at[core, b], wsem, b, sib))
        beside[b].start()
    for b in range(2):
        prod = rotateds[b] * setups[b][0]
        for p in range(pair):
            row = jnp.sum(prod[p * VP : (p + 1) * VP], axis=0, keepdims=True)
            prow[core, b * pair + p : b * pair + p + 1, :] = row
    pcopies = [remote(prow.at[core], prow.at[core], psem, 0, sib)]
    for c in pcopies:
        c.start()
    for c in beside:
        c.wait_recv()
    pending += beside + pcopies

    for f in range(4):
        wt[..., f * own : (f + 1) * own] = wbuf[f % 2, f // 2].reshape(wt.shape[:3] + (own,))
    def fill(a, o):
        rows, out, cols = ((wt, ta, slice(0, half)), (wtb, tb, slice(half, ncode)))[a]
        v = mm(rows[:, planes[o]].reshape(rank // nx, flat), mk[:, :, cols].reshape(flat, half))
        out[:, planes[o]] = v.reshape(out.shape[0], out.shape[2], half)

    terms = (ta, tb)
    coded = ((qs_a, qr_a), (qs_b, qr_b))
    live = {}

    def send_sum(a, o, e, dest, step, extra):
        qs, qr = coded[a]
        v = terms[a][dest, planes[o]]
        for other in extra:
            live[a, o, other].wait_recv()
            v = v + values_of(qr[o, other])
        qs[o, e] = to_i16(codes_of(v))
        copy = remote(qs.at[o, e], qr.at[o, e], rsem, (a * 2 + o) * 8 + e, axes[a][3](-step))
        copy.start()
        live[a, o, e] = copy
        pending.append(copy)

    def leaves(a, o):
        _, me, n, _ = axes[a]
        first, later = tree(n, 1 - 2 * o)
        for e, (k, step) in enumerate(later):
            send_sum(a, o, len(first) + e, (me - k - step + n) % n, step, ())

    def inner(a, o, ready):
        _, me, n, _ = axes[a]
        first, later = tree(n, 1 - 2 * o)
        for e, k in enumerate(first):
            extra = [len(first) + ee for ee, (kk, _) in enumerate(later) if kk == k]
            if ready != bool(extra):
                send_sum(a, o, e, (me - k + n) % n, k, extra)

    def total(a, o):
        _, me, n, _ = axes[a]
        v = terms[a][me, planes[o]]
        for e in range(len(tree(n, 1)[0])):
            live[a, o, e].wait_recv()
            v = v + values_of(coded[a][1][o, e])
        return v

    fill(0, 1)
    leaves(0, 1)
    wtb[...] = mm(to_b[...], wt[...].reshape(rank, flat)).astype(BF16).reshape(wtb.shape)
    fill(1, 1)
    leaves(1, 1)
    for a in (0, 1):
        inner(a, 1, True)
    for a in (0, 1):
        fill(a, 0)
        leaves(a, 0)
    for a in (0, 1):
        inner(a, 1, False)
    for a in (0, 1):
        inner(a, 0, True)
    for a in (0, 1):
        inner(a, 0, False)
    xsums = ((xs_a, xr_a), (xs_b, xr_b))
    xback = []
    for a in (0, 1):
        xsums[a][0][...] = to_i16(codes_of(total(a, 1)))
        xback.append(remote(xsums[a][0], xsums[a][1], xfsem, a, xdev))
        xback[a].start()
    owns = [total(a, 0) for a in (0, 1)]
    pending += xback
    last = []
    for a, (buf, got, dev, base) in enumerate(((s2a, r2a, ydev, 0), (s2b, r2b, zdev, ny))):
        xback[a].wait_recv()
        count, me = buf.shape[0], (y, z)[a]
        rel[0 : 2 * count, :] = codes_of(owns[a] + values_of(xsums[a][1][...]))
        for s in range(count):
            buf[s] = to_i16(rel[2 * s : 2 * s + 2, :])
        copies = []
        for d in range(1, count):
            copies.append(remote(buf.at[(me + d) % count], got.at[me], g2sem, base + d, dev(d)))
            copies[-1].start()
        last.append(copies)
        pending += copies
    for c in pcopies:
        c.wait_recv()
    for f in range(4):
        out_pat[f * pair : (f + 1) * pair, :] = prow[f % 2, f // 2 * pair : (f // 2 + 1) * pair]
    for a, (buf, got) in enumerate(((s2a, r2a), (s2b, r2b))):
        count, me = buf.shape[0], (y, z)[a]
        for c in last[a]:
            c.wait_recv()
        v = values_of(buf[me])
        for d in range(1, count):
            v = v + values_of(got[(me + d) % count])
        out_codes[:, a * half : (a + 1) * half] = v
    for c in pending:
        c.wait_send()


def per_device(visits, tile_pattern, counts, codes_t, core, patient_weights, dims):
    nz, nx, ny = dims
    npat, nvis, ncode = visits.shape
    rank = core.shape[0]
    half = ncode // 2
    rows_a, rows_b = 2 * nx * ny, 2 * nz * nx
    flat = npat * VP
    own = flat // 4
    dma = pltpu.SemaphoreType.DMA
    vmem = pl.BlockSpec(memory_space=pltpu.VMEM)
    scratch = [
        pltpu.VMEM((npat, nvis, ncode), BF16),
        pltpu.SMEM(tile_pattern.shape, jnp.int32),
        pltpu.SMEM(counts.shape, jnp.int32),
        pltpu.VMEM(core.shape, BF16),
        pltpu.VMEM(patient_weights.shape, F32),
        pltpu.VMEM((npat, VP, ncode), BF16),
        pltpu.VMEM((2, ncode), BF16),
        pltpu.VMEM((ny, 2, half), BF16),
        pltpu.VMEM((nz, 2, half), BF16),
        pltpu.VMEM((2, ncode), BF16),
        pltpu.VMEM((ny, 2, half), BF16),
        pltpu.VMEM((nz, 2, half), BF16),
        pltpu.VMEM((max(rows_a, rows_b), half + 128), F32),
        pltpu.VMEM((nz, 2, rows_a // 2, half), BF16),
        pltpu.VMEM((ny, 2, rows_b // 2, half), BF16),
        pltpu.VMEM((2, 2, own, rank), F32),
        pltpu.VMEM((2, own, rank), F32),
        pltpu.VMEM((2, own, rank), I16),
        pltpu.VMEM((2, own, rank), I16),
        pltpu.VMEM((2, 2, rank, own), BF16),
        pltpu.VMEM((2, npat // 2, rank), F32),
        pltpu.VMEM((nz, nx, rows_a // 2, flat), BF16),
        pltpu.VMEM((ny, nx, rows_b // 2, flat), BF16),
        pltpu.VMEM((rank, rank), BF16),
        pltpu.VMEM((rank, rank), BF16),
        pltpu.VMEM((nz, 2, rows_a // 2, half), F32),
        pltpu.VMEM((ny, 2, rows_b // 2, half), F32),
        pltpu.VMEM((2, 8, rows_a // 2, half + 128), I16),
        pltpu.VMEM((2, 8, rows_a // 2, half + 128), I16),
        pltpu.VMEM((2, 8, rows_b // 2, half + 128), I16),
        pltpu.VMEM((2, 8, rows_b // 2, half + 128), I16),
        pltpu.VMEM((ny, 2, half + 128), I16),
        pltpu.VMEM((ny, 2, half + 128), I16),
        pltpu.VMEM((nz, 2, half + 128), I16),
        pltpu.VMEM((nz, 2, half + 128), I16),
        pltpu.VMEM((rows_a // 2, half + 128), I16),
        pltpu.VMEM((rows_a // 2, half + 128), I16),
        pltpu.VMEM((rows_b // 2, half + 128), I16),
        pltpu.VMEM((rows_b // 2, half + 128), I16),
        dma((6,)),
        dma((2, 1)),
        dma((2, 2 * (ny + nz))),
        dma((2, 32)),
        dma((2, 4)),
        dma((2, 2)),
        dma((2, 1)),
        dma((2, 32)),
        dma((2, ny + nz)),
        dma((2, 2)),
    ]
    return pl.pallas_call(
        functools.partial(kernel, dims),
        out_shape=(
            jax.ShapeDtypeStruct(codes_t.shape, F32),
            jax.ShapeDtypeStruct(patient_weights.shape, F32),
        ),
        in_specs=[pl.BlockSpec(memory_space=pltpu.HBM)] * 6,
        out_specs=(vmem, vmem),
        scratch_shapes=scratch,
        compiler_params=pltpu.CompilerParams(
            collective_id=0, has_side_effects=True, vmem_limit_bytes=60 * 1024 * 1024
        ),
        name="sweep",
    )(visits, tile_pattern, counts, codes_t, core, patient_weights)


def build(mesh, dims):
    return jax.shard_map(
        functools.partial(per_device, dims=dims),
        mesh=mesh,
        in_specs=(
            P("subj", None, "feat"),
            P("subj", "feat"),
            P("subj"),
            P("subj", "feat"),
            P(),
            P("subj", None),
        ),
        out_specs=(P("subj", "feat"), P("subj", None)),
        check_vma=False,
    )


def solution(mesh):
    return build(mesh, (NZ, NX, NY))
```
